128 devices in a mesh: row: 8 (over z_lo, x), col: 16 (over z_hi, y, core).
Axes of the slice: x: 4, y: 4, z: 4 (z_hi: 2, z_lo: 2; z = z_hi * 2 + z_lo), core: 2. Of those that a mesh axis runs over, the one named last changes fastest.
Arguments:
- trunk: bfloat16 [2048, 256], P(('row', 'col')), may hold values from -6 to 6
- row_weight: bfloat16 [256, 512], replicated, may hold values from -0.375 to 0.375
- column_weight: bfloat16 [256, 512], replicated, may hold values from -0.375 to 0.375
- pair_map_weight: bfloat16 [512, 48], replicated, may hold values from -0.25 to 0.25
- dilated_weight: bfloat16 [3, 3, 48, 48], replicated, may hold values from -0.3125 to 0.3125
- mixing_weight: bfloat16 [48, 48], replicated, may hold values from -0.875 to 0.875
Outputs:
- block_out: bfloat16 [48, 2048, 2048], P(None, 'row', 'col')
The draws below stay inside these ranges and needn't reach their ends.
All inputs are finite; a program needn't handle non-finite values.
Results may differ from the reference program's by a relative error of at most 0.0067.
Values may be sent and summed in bfloat16 or wider, within the bound.
A program may use at most 128 MiB of HBM per device.

```python
import jax
import jax.numpy as jnp
from jax import lax

TRUNK = 256
PAIR = 512
MAP_CHANNELS = 48
DILATION_STEP = 8
REGION_BINS = 2048


def level_of(key, extent, pieces, low, top_value):
    def one(axis_at, shards_of):
        draws = jax.random.uniform(jax.random.fold_in(jax.random.fold_in(key, 6), axis_at), (shards_of,), jnp.float32, low / len(pieces), top_value / len(pieces))
        return jnp.repeat(jnp.exp(draws), extent[axis_at] // shards_of).reshape((-1,) + (1,) * (len(extent) - axis_at - 1))

    gain = one(*pieces[0])
    for cut in pieces[1:]:
        gain = gain * one(*cut)
    return gain


def bell_draw(key, dims, scale, limit, cuts=(), kind=jnp.bfloat16):
    drawn = scale * jax.random.normal(key, dims, jnp.float32)
    if cuts:
        drawn = drawn * level_of(key, dims, cuts, -0.22, 0.18)
    return jnp.clip(drawn, -limit, limit).astype(kind)


def setup_inputs(seed: int = 0) -> dict:
    key_of = jax.random.split(jax.random.key(seed), 7)
    return {
        "trunk": bell_draw(key_of[0], (REGION_BINS, TRUNK), 1.0, 6.0, ((0, 128),)),
        "row_weight": bell_draw(key_of[1], (TRUNK, PAIR), TRUNK ** -0.5, 0.375),
        "column_weight": bell_draw(key_of[2], (TRUNK, PAIR), TRUNK ** -0.5, 0.375),
        "pair_map_weight": bell_draw(key_of[3], (PAIR, MAP_CHANNELS), PAIR ** -0.5, 0.25),
        "dilated_weight": bell_draw(key_of[4], (3, 3, MAP_CHANNELS, MAP_CHANNELS), (9 * MAP_CHANNELS) ** -0.5, 0.3125),
        "mixing_weight": bell_draw(key_of[5], (MAP_CHANNELS, MAP_CHANNELS), MAP_CHANNELS ** -0.5, 0.875),
    }


def reference(trunk, row_weight, column_weight, pair_map_weight, dilated_weight, mixing_weight):
    row_proj = jnp.dot(trunk, row_weight, preferred_element_type=jnp.float32).astype(jnp.bfloat16)
    col_proj = jnp.dot(trunk, column_weight, preferred_element_type=jnp.float32).astype(jnp.bfloat16)
    col_wide = col_proj.astype(jnp.float32)
    pair_weight = pair_map_weight.astype(jnp.float32)
    blocksz = min(16, REGION_BINS)
    count = REGION_BINS // blocksz

    def pair_rows(rows):
        summed = rows.astype(jnp.float32)[:, None, :] + col_wide[None, :, :]
        pair_act = jnp.maximum(summed, 0.0).astype(jnp.bfloat16)
        hidden = jnp.einsum('ijk,ko->oij', pair_act.astype(jnp.float32), pair_weight)
        return hidden.astype(jnp.bfloat16)

    stacked = lax.map(pair_rows, row_proj.reshape(count, blocksz, PAIR))
    base = jnp.transpose(stacked, (1, 0, 2, 3)).reshape(MAP_CHANNELS, REGION_BINS, REGION_BINS)
    pair_activation = jnp.maximum(base, jnp.zeros((), jnp.bfloat16))
    padded_pairs = jnp.pad(pair_activation, ((0, 0), (DILATION_STEP, DILATION_STEP), (DILATION_STEP, DILATION_STEP)))
    dilated_kernel_weight = dilated_weight.astype(jnp.float32)
    mix_weight = mixing_weight.astype(jnp.float32)
    row_block_slice = min(256, REGION_BINS)
    nblocks = REGION_BINS // row_block_slice

    def conv_rows(start_index):
        start_index = start_index.astype(jnp.int32)
        total_sum = jnp.zeros((MAP_CHANNELS, row_block_slice, REGION_BINS), jnp.float32)
        for first_tap_offset in range(3):
            for second_tap_offset in range(3):
                neighbour_window = lax.dynamic_slice(padded_pairs, (jnp.int32(0), start_index + first_tap_offset * DILATION_STEP, jnp.int32(second_tap_offset * DILATION_STEP)), (MAP_CHANNELS, row_block_slice, REGION_BINS))
                total_sum = total_sum + jnp.einsum('zy,yea->zea', dilated_kernel_weight[first_tap_offset, second_tap_offset], neighbour_window.astype(jnp.float32))
        mid = jnp.maximum(total_sum, 0.0).astype(jnp.bfloat16)
        here = lax.dynamic_slice(base, (jnp.int32(0), start_index, jnp.int32(0)), (MAP_CHANNELS, row_block_slice, REGION_BINS))
        result = here.astype(jnp.float32) + jnp.einsum('zy,yea->zea', mix_weight, mid.astype(jnp.float32))
        return result.astype(jnp.bfloat16)

    starts = (jnp.arange(nblocks) * row_block_slice).astype(jnp.int32)
    outblk = lax.map(conv_rows, starts)
    return jnp.transpose(outblk, (1, 0, 2, 3)).reshape(MAP_CHANNELS, REGION_BINS, REGION_BINS)
```

```python
import jax
import jax.numpy as jnp
from jax import lax
from jax.experimental import pallas as pl
from jax.experimental.pallas import tpu as pltpu
from jax.sharding import PartitionSpec as P

bf16 = jnp.bfloat16
f32 = jnp.float32
MESH = pl.DeviceIdType.MESH
VMEM = pl.BlockSpec(memory_space=pltpu.VMEM)


def gather_kernel(x_ref, rows_ref, cols_ref, zero_ref, send_sem, rows_sem, cols_sem):
    r = lax.axis_index("row")
    c = lax.axis_index("col")
    k = lax.rem(c, 8)
    home = 2 * r + c // 8
    barrier = pltpu.get_barrier_semaphore()
    zero_ref[...] = jnp.zeros_like(zero_ref)

    def signal(row, col):
        pl.semaphore_signal(barrier, inc=1, device_id=(row, col), device_id_type=MESH)

    def each(count, body):
        def step(n, carry):
            body(n)
            return carry

        lax.fori_loop(0, count, step, 0)

    each(15, lambda n: signal(r, lax.rem(c + 1 + n, 16)))

    @pl.when(r > 0)
    def _():
        signal(r - 1, 15)

    @pl.when(r < 7)
    def _():
        signal(r + 1, 0)

    def signal_column_source(n):
        row, col = c // 2, 8 * lax.rem(c, 2) + n

        @pl.when((row != r) | (col != c))
        def _():
            signal(row, col)

    each(8, signal_column_source)

    @pl.when(c > 0)
    def _():
        row, col = (c - 1) // 2, 8 * lax.rem(c - 1, 2) + 7

        @pl.when((row != r) | (col != c))
        def _():
            signal(row, col)

    @pl.when(c < 15)
    def _():
        row, col = (c + 1) // 2, 8 * lax.rem(c + 1, 2)

        @pl.when((row != r) | (col != c))
        def _():
            signal(row, col)

    low_halo_rows = (c == 15) & (r < 7)
    high_halo_rows = (c == 0) & (r > 0)
    low_halo_cols = (k == 7) & (home < 15)
    high_halo_cols = (k == 0) & (home > 0)

    def away(col):
        return 7 + (col != c).astype(jnp.int32)

    peers = 15 + away(home)
    peers += 16 * (low_halo_rows | high_halo_rows).astype(jnp.int32)
    peers += low_halo_cols.astype(jnp.int32) * away(home + 1)
    peers += high_halo_cols.astype(jnp.int32) * away(home - 1)
    pl.semaphore_wait(barrier, peers)

    def remote(src, dst, sem, row, col):
        return pltpu.make_async_remote_copy(
            src_ref=src, dst_ref=dst, send_sem=send_sem, recv_sem=sem, device_id=(row, col), device_id_type=MESH
        )

    own_rows = rows_ref.at[pl.ds(1 + 2 * c, 2)]
    own_cols = cols_ref.at[pl.ds(1 + 2 * k, 2)]

    def to_column(src, dst, col):
        def body(n):
            row = lax.rem(r + n, 8)
            other = (row != r) | (col != c)

            @pl.when(other)
            def _():
                remote(src, dst, cols_sem, row, col).start()

            @pl.when(jnp.logical_not(other))
            def _():
                pltpu.make_async_copy(src, dst, cols_sem).start()

        each(8, body)

    @pl.when(low_halo_rows)
    def _():
        each(16, lambda n: remote(x_ref.at[1], rows_ref.at[0], rows_sem, r + 1, n).start())

    @pl.when(high_halo_rows)
    def _():
        each(16, lambda n: remote(x_ref.at[0], rows_ref.at[33], rows_sem, r - 1, n).start())

    @pl.when(low_halo_cols)
    def _():
        to_column(x_ref.at[1], cols_ref.at[0], home + 1)

    @pl.when(high_halo_cols)
    def _():
        to_column(x_ref.at[0], cols_ref.at[17], home - 1)

    to_column(x_ref, own_cols, home)
    each(15, lambda n: remote(x_ref, own_rows, rows_sem, r, lax.rem(c + 1 + n, 16)).start())
    pltpu.make_async_copy(x_ref, own_rows, rows_sem).start()

    @pl.when(r == 0)
    def _():
        pltpu.make_async_copy(zero_ref, rows_ref.at[0], rows_sem).start()

    @pl.when(r == 7)
    def _():
        pltpu.make_async_copy(zero_ref, rows_ref.at[33], rows_sem).start()

    @pl.when(c == 0)
    def _():
        pltpu.make_async_copy(zero_ref, cols_ref.at[0], cols_sem).start()

    @pl.when(c == 15)
    def _():
        pltpu.make_async_copy(zero_ref, cols_ref.at[17], cols_sem).start()

    def sent(blocks):
        part = rows_ref.at[pl.ds(0, blocks)]
        pltpu.make_async_copy(part, part, send_sem).wait()

    sent(30)

    sent(14)

    @pl.when(home != c)
    def _():
        sent(2)

    @pl.when(low_halo_rows)
    def _():
        sent(16)

    @pl.when(high_halo_rows)
    def _():
        sent(16)

    def column_sent(col):
        sent(7)

        @pl.when(col != c)
        def _():
            sent(1)

    @pl.when(low_halo_cols)
    def _():
        column_sent(home + 1)

    @pl.when(high_halo_cols)
    def _():
        column_sent(home - 1)

    pltpu.make_async_copy(rows_ref, rows_ref, rows_sem).wait()
    pltpu.make_async_copy(cols_ref, cols_ref, cols_sem).wait()


def gather(trunk):
    width = trunk.shape[1]
    return pl.pallas_call(
        gather_kernel,
        out_shape=(
            jax.ShapeDtypeStruct((34, 8, width), bf16),
            jax.ShapeDtypeStruct((18, 8, width), bf16),
        ),
        in_specs=[VMEM],
        out_specs=(VMEM, VMEM),
        scratch_shapes=[
            pltpu.VMEM((8, width), bf16),
            pltpu.SemaphoreType.DMA,
            pltpu.SemaphoreType.DMA,
            pltpu.SemaphoreType.DMA,
        ],
        compiler_params=pltpu.CompilerParams(collective_id=0, has_side_effects=True),
        name="gather_bins",
    )(trunk.reshape(2, 8, width))


def dot(a, b, dims=((1,), (0,))):
    return lax.dot_general(a, b, (dims, ((), ())), preferred_element_type=f32)


def block_kernel(
    rows_ref, cols_ref, row_w_ref, col_w_ref, pair_w_ref, taps_ref, mix_ref, out_ref, row_pat, col_pat, act, base, taps, turn
):
    r = lax.axis_index("row")
    c = lax.axis_index("col")
    row_w = row_w_ref[...].T
    col_w = col_w_ref[...].T
    pair_w = pair_w_ref[...].T
    for a in range(3):
        for b in range(3):
            taps[48 * b : 48 * b + 48, 48 * a : 48 * a + 48] = taps_ref[a, b]
    for n in range(9):
        row_cells = []
        col_cells = []
        for p in (2 * n, 2 * n + 1):
            for e in range(2):
                bins = rows_ref[16 * e + p].astype(f32)
                row_cells.append(jnp.broadcast_to(bins[:, None, :], (8, 8, 256)).reshape(64, 256))
            bins = cols_ref[p].astype(f32)
            col_cells.append(jnp.broadcast_to(bins[None], (16, 8, 256)).reshape(128, 256))
        proj = dot(row_w, jnp.concatenate(row_cells, 0).astype(bf16), ((1,), (1,))).astype(bf16)
        row_pat[2 * n] = proj[:, :128]
        row_pat[2 * n + 1] = proj[:, 128:]
        proj = dot(col_w, jnp.concatenate(col_cells, 0).astype(bf16), ((1,), (1,))).astype(bf16)
        col_pat[2 * n] = proj[:, :128]
        col_pat[2 * n + 1] = proj[:, 128:]

    lane = lax.broadcasted_iota(jnp.int32, (1, 128), 1)
    zero = jnp.zeros((), bf16)

    def pair_rows(p, carry):
        row = row_pat[p]
        tile_row = 32 * r + 16 * (lane // 64) + p - 1
        inside = ((tile_row >= 0) & (tile_row < 256)).astype(f32)
        first = inside * (c > 0).astype(f32)
        last = inside * (c < 15).astype(f32)
        at = pl.ds(pl.multiple_of(48 * p, 16), 48)
        for n in range(9):
            pair_act = jnp.concatenate(
                [jnp.maximum(row + col_pat[2 * n], zero), jnp.maximum(row + col_pat[2 * n + 1], zero)], axis=1
            )
            hidden = dot(pair_w, pair_act)
            keep = jnp.concatenate([first if n == 0 else inside, last if n == 8 else inside], axis=1)
            act[at, 256 * n : 256 * n + 256] = (jnp.maximum(hidden, 0.0) * keep).astype(bf16)
            base[at, 256 * n : 256 * n + 256] = hidden.astype(bf16)
        return carry

    lax.fori_loop(0, 18, pair_rows, 0)

    mix = mix_ref[...]
    tap_w = taps[...]
    group = lane // 8

    def conv_rows(m, carry):
        for u in range(2):
            p = 2 * m + u
            at = pl.ds(pl.multiple_of(48 * p, 16), 144)
            parts = [dot(tap_w, act[at, 256 * n : 256 * n + 256]) for n in range(9)]

            def part(b, q):
                return parts[q // 2][48 * b : 48 * b + 48, 128 * (q % 2) : 128 * (q % 2) + 128]

            tiles = []
            for n in range(8):
                mids = [
                    jnp.maximum(part(0, q - 1) + part(1, q) + part(2, q + 1), 0.0).astype(bf16)
                    for q in (2 * n + 1, 2 * n + 2)
                ]
                here = base[pl.ds(pl.multiple_of(48 * (p + 1), 16), 48), 256 * n + 128 : 256 * n + 384]
                cells = (dot(mix, jnp.concatenate(mids, axis=1)) + here.astype(f32)).astype(bf16)
                tiles += [cells[:, :128], cells[:, 128:]]
            for d in (1, 2, 4, 8):
                stay = (group & d) == 0
                for q in range(16):
                    if q & d == 0:
                        x, y = tiles[q], tiles[q + d]
                        tiles[q] = jnp.where(stay, x, pltpu.roll(y, 8 * d, 1))
                        tiles[q + d] = jnp.where(stay, pltpu.roll(x, 128 - 8 * d, 1), y)
            for k in range(16):
                turn[k // 8, pl.ds(8 * u + k % 8, 48, stride=16), :] = tiles[k].astype(f32)
        for e in range(2):
            out_ref[:, pl.ds(pl.multiple_of(128 * e + 16 * m, 16), 16), :] = turn[e].reshape(48, 16, 128).astype(bf16)
        return carry

    lax.fori_loop(0, 8, conv_rows, 0)


def on_device(trunk, row_weight, column_weight, pair_map_weight, dilated_weight, mixing_weight):
    rows, cols = gather(trunk)
    return pl.pallas_call(
        block_kernel,
        out_shape=jax.ShapeDtypeStruct((48, 256, 128), bf16),
        in_specs=[VMEM] * 7,
        out_specs=VMEM,
        scratch_shapes=[
            pltpu.VMEM((18, 512, 128), bf16),
            pltpu.VMEM((18, 512, 128), bf16),
            pltpu.VMEM((18 * 48, 18 * 128), bf16),
            pltpu.VMEM((18 * 48, 18 * 128), bf16),
            pltpu.VMEM((144, 144), bf16),
            pltpu.VMEM((2, 768, 128), f32),
        ],
        compiler_params=pltpu.CompilerParams(vmem_limit_bytes=48 << 20),
        name="pair_block",
    )(rows, cols, row_weight, column_weight, pair_map_weight, dilated_weight, mixing_weight)


def solution(mesh):
    return jax.shard_map(
        on_device,
        mesh=mesh,
        in_specs=(P(("row", "col"), None), P(), P(), P(), P(), P()),
        out_specs=P(None, "row", "col"),
        check_vma=False,
    )
```

```python
import jax
import jax.numpy as jnp
from jax import lax
from jax.experimental import pallas as pl
from jax.experimental.pallas import tpu as pltpu
from jax.sharding import PartitionSpec as P

bf16 = jnp.bfloat16
f32 = jnp.float32
MESH = pl.DeviceIdType.MESH
VMEM = pl.BlockSpec(memory_space=pltpu.VMEM)


def gather_kernel(x_ref, rows_ref, cols_ref, zero_ref, send_sem, rows_sem, cols_sem):
    r = lax.axis_index("row")
    c = lax.axis_index("col")
    k = lax.rem(c, 8)
    home = 2 * r + c // 8
    barrier = pltpu.get_barrier_semaphore()
    zero_ref[...] = jnp.zeros_like(zero_ref)

    def signal(row, col):
        pl.semaphore_signal(barrier, inc=1, device_id=(row, col), device_id_type=MESH)

    def each(count, body):
        def step(n, carry):
            body(n)
            return carry

        lax.fori_loop(0, count, step, 0)

    each(15, lambda n: signal(r, lax.rem(c + 1 + n, 16)))

    @pl.when(r > 0)
    def _():
        signal(r - 1, 15)

    @pl.when(r < 7)
    def _():
        signal(r + 1, 0)

    def signal_column_source(n):
        row, col = c // 2, 8 * lax.rem(c, 2) + n

        @pl.when((row != r) | (col != c))
        def _():
            signal(row, col)

    each(8, signal_column_source)

    @pl.when(c > 0)
    def _():
        row, col = (c - 1) // 2, 8 * lax.rem(c - 1, 2) + 7

        @pl.when((row != r) | (col != c))
        def _():
            signal(row, col)

    @pl.when(c < 15)
    def _():
        row, col = (c + 1) // 2, 8 * lax.rem(c + 1, 2)

        @pl.when((row != r) | (col != c))
        def _():
            signal(row, col)

    low_halo_rows = (c == 15) & (r < 7)
    high_halo_rows = (c == 0) & (r > 0)
    low_halo_cols = (k == 7) & (home < 15)
    high_halo_cols = (k == 0) & (home > 0)

    def away(col):
        return 7 + (col != c).astype(jnp.int32)

    peers = 15 + away(home)
    peers += 16 * (low_halo_rows | high_halo_rows).astype(jnp.int32)
    peers += low_halo_cols.astype(jnp.int32) * away(home + 1)
    peers += high_halo_cols.astype(jnp.int32) * away(home - 1)
    pl.semaphore_wait(barrier, peers)

    def remote(src, dst, sem, row, col):
        return pltpu.make_async_remote_copy(
            src_ref=src, dst_ref=dst, send_sem=send_sem, recv_sem=sem, device_id=(row, col), device_id_type=MESH
        )

    own_rows = rows_ref.at[pl.ds(1 + 2 * c, 2)]
    own_cols = cols_ref.at[pl.ds(1 + 2 * k, 2)]

    def to_column(src, dst, col):
        def body(n):
            row = lax.rem(r + n, 8)
            other = (row != r) | (col != c)

            @pl.when(other)
            def _():
                remote(src, dst, cols_sem, row, col).start()

            @pl.when(jnp.logical_not(other))
            def _():
                pltpu.make_async_copy(src, dst, cols_sem).start()

        each(8, body)

    @pl.when(low_halo_rows)
    def _():
        each(16, lambda n: remote(x_ref.at[1], rows_ref.at[0], rows_sem, r + 1, n).start())

    @pl.when(high_halo_rows)
    def _():
        each(16, lambda n: remote(x_ref.at[0], rows_ref.at[33], rows_sem, r - 1, n).start())

    @pl.when(low_halo_cols)
    def _():
        to_column(x_ref.at[1], cols_ref.at[0], home + 1)

    @pl.when(high_halo_cols)
    def _():
        to_column(x_ref.at[0], cols_ref.at[17], home - 1)

    to_column(x_ref, own_cols, home)
    each(15, lambda n: remote(x_ref, own_rows, rows_sem, r, lax.rem(c + 1 + n, 16)).start())
    pltpu.make_async_copy(x_ref, own_rows, rows_sem).start()

    @pl.when(r == 0)
    def _():
        pltpu.make_async_copy(zero_ref, rows_ref.at[0], rows_sem).start()

    @pl.when(r == 7)
    def _():
        pltpu.make_async_copy(zero_ref, rows_ref.at[33], rows_sem).start()

    @pl.when(c == 0)
    def _():
        pltpu.make_async_copy(zero_ref, cols_ref.at[0], cols_sem).start()

    @pl.when(c == 15)
    def _():
        pltpu.make_async_copy(zero_ref, cols_ref.at[17], cols_sem).start()

    def sent(blocks):
        part = rows_ref.at[pl.ds(0, blocks)]
        pltpu.make_async_copy(part, part, send_sem).wait()

    sent(30)

    sent(14)

    @pl.when(home != c)
    def _():
        sent(2)

    @pl.when(low_halo_rows)
    def _():
        sent(16)

    @pl.when(high_halo_rows)
    def _():
        sent(16)

    def column_sent(col):
        sent(7)

        @pl.when(col != c)
        def _():
            sent(1)

    @pl.when(low_halo_cols)
    def _():
        column_sent(home + 1)

    @pl.when(high_halo_cols)
    def _():
        column_sent(home - 1)

    pltpu.make_async_copy(rows_ref, rows_ref, rows_sem).wait()
    pltpu.make_async_copy(cols_ref, cols_ref, cols_sem).wait()


def gather(trunk):
    width = trunk.shape[1]
    return pl.pallas_call(
        gather_kernel,
        out_shape=(
            jax.ShapeDtypeStruct((34, 8, width), bf16),
            jax.ShapeDtypeStruct((18, 8, width), bf16),
        ),
        in_specs=[VMEM],
        out_specs=(VMEM, VMEM),
        scratch_shapes=[
            pltpu.VMEM((8, width), bf16),
            pltpu.SemaphoreType.DMA,
            pltpu.SemaphoreType.DMA,
            pltpu.SemaphoreType.DMA,
        ],
        compiler_params=pltpu.CompilerParams(collective_id=0, has_side_effects=True),
        name="gather_bins",
    )(trunk.reshape(2, 8, width))


def dot(a, b, dims=((1,), (0,))):
    return lax.dot_general(a, b, (dims, ((), ())), preferred_element_type=f32)


def block_kernel(
    rows_hbm, cols_hbm, row_w_hbm, col_w_hbm, pair_w_hbm, taps_hbm, mix_hbm, out_hbm,
    rows_in, cols_in, row_w_in, col_w_in, pair_w_in, taps_in, mix_in,
    row_pat, col_pat, act, base, taps, turn, out_tile, in_sem, out_sem,
):
    r = lax.axis_index("row")
    c = lax.axis_index("col")
    loads = [
        pltpu.make_async_copy(src, dst, in_sem.at[n])
        for n, (src, dst) in enumerate(
            (
                (row_w_hbm, row_w_in),
                (rows_hbm, rows_in),
                (col_w_hbm, col_w_in),
                (cols_hbm, cols_in),
                (taps_hbm, taps_in),
                (pair_w_hbm, pair_w_in),
                (mix_hbm, mix_in),
            )
        )
    ]
    for load in loads:
        load.start()

    loads[0].wait()
    row_w = row_w_in[...].T
    loads[1].wait()
    for n in range(9):
        cells = []
        for p in (2 * n, 2 * n + 1):
            for e in range(2):
                bins = rows_in[16 * e + p].astype(f32)
                cells.append(jnp.broadcast_to(bins[:, None, :], (8, 8, 256)).reshape(64, 256))
        proj = dot(row_w, jnp.concatenate(cells, 0).astype(bf16), ((1,), (1,))).astype(bf16)
        row_pat[2 * n] = proj[:, :128]
        row_pat[2 * n + 1] = proj[:, 128:]
    loads[2].wait()
    col_w = col_w_in[...].T
    loads[3].wait()
    for n in range(9):
        cells = [jnp.broadcast_to(cols_in[q].astype(f32)[None], (16, 8, 256)).reshape(128, 256) for q in (2 * n, 2 * n + 1)]
        proj = dot(col_w, jnp.concatenate(cells, 0).astype(bf16), ((1,), (1,))).astype(bf16)
        col_pat[2 * n] = proj[:, :128]
        col_pat[2 * n + 1] = proj[:, 128:]
    loads[4].wait()
    for a in range(3):
        for b in range(3):
            taps[48 * b : 48 * b + 48, 48 * a : 48 * a + 48] = taps_in[a, b]
    loads[5].wait()
    loads[6].wait()

    lane = lax.broadcasted_iota(jnp.int32, (1, 128), 1)
    zero = jnp.zeros((), bf16)
    pair_w = pair_w_in[...]

    def pair_rows(p, carry):
        row = row_pat[p]
        tile_row = 32 * r + 16 * (lane // 64) + p - 1
        inside = ((tile_row >= 0) & (tile_row < 256)).astype(f32)
        first = inside * (c > 0).astype(f32)
        last = inside * (c < 15).astype(f32)
        at = pl.ds(pl.multiple_of(48 * p, 16), 48)
        for n in range(9):
            pair_act = jnp.concatenate(
                [jnp.maximum(row + col_pat[2 * n], zero), jnp.maximum(row + col_pat[2 * n + 1], zero)], axis=1
            )
            hidden = dot(pair_w, pair_act)
            keep = jnp.concatenate([first if n == 0 else inside, last if n == 8 else inside], axis=1)
            act[at, 256 * n : 256 * n + 256] = (jnp.maximum(hidden, 0.0) * keep).astype(bf16)
            base[at, 256 * n : 256 * n + 256] = hidden.astype(bf16)
        return carry

    lax.fori_loop(0, 18, pair_rows, 0)

    mix = mix_in[...]
    tap_w = taps[...]
    group = lane // 8

    def store(slot, e, m):
        return pltpu.make_async_copy(
            out_tile.at[slot, e], out_hbm.at[:, pl.ds(pl.multiple_of(128 * e + 16 * m, 16), 16), :], out_sem.at[slot, e]
        )

    def conv_rows(m, carry):
        slot = lax.rem(m, 2)
        for u in range(2):
            p = 2 * m + u
            at = pl.ds(pl.multiple_of(48 * p, 16), 144)
            parts = [dot(tap_w, act[at, 256 * n : 256 * n + 256]) for n in range(9)]

            def part(b, q):
                return parts[q // 2][48 * b : 48 * b + 48, 128 * (q % 2) : 128 * (q % 2) + 128]

            tiles = []
            for n in range(8):
                mids = [
                    jnp.maximum(part(0, q - 1) + part(1, q) + part(2, q + 1), 0.0).astype(bf16)
                    for q in (2 * n + 1, 2 * n + 2)
                ]
                here = base[pl.ds(pl.multiple_of(48 * (p + 1), 16), 48), 256 * n + 128 : 256 * n + 384]
                cells = (dot(mix, jnp.concatenate(mids, axis=1)) + here.astype(f32)).astype(bf16)
                tiles += [cells[:, :128], cells[:, 128:]]
            for d in (1, 2, 4, 8):
                stay = (group & d) == 0
                for q in range(16):
                    if q & d == 0:
                        x, y = tiles[q], tiles[q + d]
                        tiles[q] = jnp.where(stay, x, pltpu.roll(y, 8 * d, 1))
                        tiles[q + d] = jnp.where(stay, pltpu.roll(x, 128 - 8 * d, 1), y)
            for k in range(16):
                turn[k // 8, pl.ds(8 * u + k % 8, 48, stride=16), :] = tiles[k].astype(f32)

        @pl.when(m >= 2)
        def _():
            for e in range(2):
                store(slot, e, m - 2).wait()

        for e in range(2):
            out_tile[slot, e] = turn[e].reshape(48, 16, 128).astype(bf16)
            store(slot, e, m).start()
        return carry

    lax.fori_loop(0, 8, conv_rows, 0)
    for m in (6, 7):
        for e in range(2):
            store(m % 2, e, m).wait()


def block(rows, cols, row_weight, column_weight, pair_map_weight, dilated_weight, mixing_weight):
    hbm = pl.BlockSpec(memory_space=pltpu.HBM)
    return pl.pallas_call(
        block_kernel,
        out_shape=jax.ShapeDtypeStruct((48, 256, 128), bf16),
        in_specs=[hbm] * 7,
        out_specs=hbm,
        scratch_shapes=[
            pltpu.VMEM((34, 8, 256), bf16),
            pltpu.VMEM((18, 8, 256), bf16),
            pltpu.VMEM((256, 512), bf16),
            pltpu.VMEM((256, 512), bf16),
            pltpu.VMEM((48, 512), bf16),
            pltpu.VMEM((3, 3, 48, 48), bf16),
            pltpu.VMEM((48, 48), bf16),
            pltpu.VMEM((18, 512, 128), bf16),
            pltpu.VMEM((18, 512, 128), bf16),
            pltpu.VMEM((18 * 48, 18 * 128), bf16),
            pltpu.VMEM((18 * 48, 18 * 128), bf16),
            pltpu.VMEM((144, 144), bf16),
            pltpu.VMEM((2, 768, 128), f32),
            pltpu.VMEM((2, 2, 48, 16, 128), bf16),
            pltpu.SemaphoreType.DMA((7,)),
            pltpu.SemaphoreType.DMA((2, 2)),
        ],
        compiler_params=pltpu.CompilerParams(vmem_limit_bytes=48 << 20),
        name="pair_block",
    )(rows, cols, row_weight, column_weight, pair_map_weight.T, dilated_weight, mixing_weight)


def on_device(trunk, row_weight, column_weight, pair_map_weight, dilated_weight, mixing_weight):
    rows, cols = gather(trunk)
    return block(rows, cols, row_weight, column_weight, pair_map_weight, dilated_weight, mixing_weight)


def solution(mesh):
    return jax.shard_map(
        on_device,
        mesh=mesh,
        in_specs=(P(("row", "col"), None), P(), P(), P(), P(), P()),
        out_specs=P(None, "row", "col"),
        check_vma=False,
    )
```

```python
import jax
import jax.numpy as jnp
from jax import lax
from jax.experimental import pallas as pl
from jax.experimental.pallas import tpu as pltpu
from jax.sharding import PartitionSpec as P

bf16 = jnp.bfloat16
f32 = jnp.float32
MESH = pl.DeviceIdType.MESH
VMEM = pl.BlockSpec(memory_space=pltpu.VMEM)


def gather_kernel(x_ref, rows_ref, cols_ref, zero_ref, send_sem, rows_sem, cols_sem):
    r = lax.axis_index("row")
    c = lax.axis_index("col")
    k = lax.rem(c, 8)
    home = 2 * r + c // 8
    barrier = pltpu.get_barrier_semaphore()
    zero_ref[...] = jnp.zeros_like(zero_ref)

    def signal(row, col):
        pl.semaphore_signal(barrier, inc=1, device_id=(row, col), device_id_type=MESH)

    def each(count, body):
        def step(n, carry):
            body(n)
            return carry

        lax.fori_loop(0, count, step, 0)

    each(15, lambda n: signal(r, lax.rem(c + 1 + n, 16)))

    @pl.when(r > 0)
    def _():
        signal(r - 1, 15)

    @pl.when(r < 7)
    def _():
        signal(r + 1, 0)

    def signal_column_source(n):
        row, col = c // 2, 8 * lax.rem(c, 2) + n

        @pl.when((row != r) | (col != c))
        def _():
            signal(row, col)

    each(8, signal_column_source)

    @pl.when(c > 0)
    def _():
        row, col = (c - 1) // 2, 8 * lax.rem(c - 1, 2) + 7

        @pl.when((row != r) | (col != c))
        def _():
            signal(row, col)

    @pl.when(c < 15)
    def _():
        row, col = (c + 1) // 2, 8 * lax.rem(c + 1, 2)

        @pl.when((row != r) | (col != c))
        def _():
            signal(row, col)

    low_halo_rows = (c == 15) & (r < 7)
    high_halo_rows = (c == 0) & (r > 0)
    low_halo_cols = (k == 7) & (home < 15)
    high_halo_cols = (k == 0) & (home > 0)

    def away(col):
        return 7 + (col != c).astype(jnp.int32)

    peers = 15 + away(home)
    peers += 16 * (low_halo_rows | high_halo_rows).astype(jnp.int32)
    peers += low_halo_cols.astype(jnp.int32) * away(home + 1)
    peers += high_halo_cols.astype(jnp.int32) * away(home - 1)
    pl.semaphore_wait(barrier, peers)

    def remote(src, dst, sem, row, col):
        return pltpu.make_async_remote_copy(
            src_ref=src, dst_ref=dst, send_sem=send_sem, recv_sem=sem, device_id=(row, col), device_id_type=MESH
        )

    own_rows = rows_ref.at[pl.ds(1 + 2 * c, 2)]
    own_cols = cols_ref.at[pl.ds(1 + 2 * k, 2)]

    def to_column(src, dst, col):
        def body(n):
            row = lax.rem(r + n, 8)
            other = (row != r) | (col != c)

            @pl.when(other)
            def _():
                remote(src, dst, cols_sem, row, col).start()

            @pl.when(jnp.logical_not(other))
            def _():
                pltpu.make_async_copy(src, dst, cols_sem).start()

        each(8, body)

    @pl.when(low_halo_rows)
    def _():
        each(16, lambda n: remote(x_ref.at[1], rows_ref.at[0], rows_sem, r + 1, n).start())

    @pl.when(high_halo_rows)
    def _():
        each(16, lambda n: remote(x_ref.at[0], rows_ref.at[33], rows_sem, r - 1, n).start())

    @pl.when(low_halo_cols)
    def _():
        to_column(x_ref.at[1], cols_ref.at[0], home + 1)

    @pl.when(high_halo_cols)
    def _():
        to_column(x_ref.at[0], cols_ref.at[17], home - 1)

    to_column(x_ref, own_cols, home)
    each(15, lambda n: remote(x_ref, own_rows, rows_sem, r, lax.rem(c + 1 + n, 16)).start())
    pltpu.make_async_copy(x_ref, own_rows, rows_sem).start()

    @pl.when(r == 0)
    def _():
        pltpu.make_async_copy(zero_ref, rows_ref.at[0], rows_sem).start()

    @pl.when(r == 7)
    def _():
        pltpu.make_async_copy(zero_ref, rows_ref.at[33], rows_sem).start()

    @pl.when(c == 0)
    def _():
        pltpu.make_async_copy(zero_ref, cols_ref.at[0], cols_sem).start()

    @pl.when(c == 15)
    def _():
        pltpu.make_async_copy(zero_ref, cols_ref.at[17], cols_sem).start()

    def sent(blocks):
        part = rows_ref.at[pl.ds(0, blocks)]
        pltpu.make_async_copy(part, part, send_sem).wait()

    sent(30)

    sent(14)

    @pl.when(home != c)
    def _():
        sent(2)

    @pl.when(low_halo_rows)
    def _():
        sent(16)

    @pl.when(high_halo_rows)
    def _():
        sent(16)

    def column_sent(col):
        sent(7)

        @pl.when(col != c)
        def _():
            sent(1)

    @pl.when(low_halo_cols)
    def _():
        column_sent(home + 1)

    @pl.when(high_halo_cols)
    def _():
        column_sent(home - 1)

    pltpu.make_async_copy(rows_ref, rows_ref, rows_sem).wait()
    pltpu.make_async_copy(cols_ref, cols_ref, cols_sem).wait()


def gather(trunk):
    width = trunk.shape[1]
    return pl.pallas_call(
        gather_kernel,
        out_shape=(
            jax.ShapeDtypeStruct((34, 8, width), bf16),
            jax.ShapeDtypeStruct((18, 8, width), bf16),
        ),
        in_specs=[VMEM],
        out_specs=(VMEM, VMEM),
        scratch_shapes=[
            pltpu.VMEM((8, width), bf16),
            pltpu.SemaphoreType.DMA,
            pltpu.SemaphoreType.DMA,
            pltpu.SemaphoreType.DMA,
        ],
        compiler_params=pltpu.CompilerParams(collective_id=0, has_side_effects=True),
        name="gather_bins",
    )(trunk.reshape(2, 8, width))


def dot(a, b, dims=((1,), (0,))):
    return lax.dot_general(a, b, (dims, ((), ())), preferred_element_type=f32)


def block_kernel(
    rows_hbm, cols_hbm, row_w_hbm, col_w_hbm, pair_w_hbm, taps_hbm, mix_hbm, out_hbm,
    rows_in, cols_in, row_w_in, col_w_in, pair_w_in, taps_in, mix_in,
    row_pat, col_pat, act, base, taps, turn, out_tile, in_sem, out_sem,
):
    r = lax.axis_index("row")
    c = lax.axis_index("col")
    loads = [
        pltpu.make_async_copy(src, dst, in_sem.at[n])
        for n, (src, dst) in enumerate(
            (
                (row_w_hbm, row_w_in),
                (rows_hbm, rows_in),
                (col_w_hbm, col_w_in),
                (cols_hbm, cols_in),
                (taps_hbm, taps_in),
                (pair_w_hbm, pair_w_in),
                (mix_hbm, mix_in),
            )
        )
    ]
    for load in loads:
        load.start()

    loads[0].wait()
    row_w = row_w_in[...].T
    loads[1].wait()
    for n in range(9):
        cells = []
        for p in (2 * n, 2 * n + 1):
            for e in range(2):
                bins = rows_in[16 * e + p].astype(f32)
                cells.append(jnp.broadcast_to(bins[:, None, :], (8, 8, 256)).reshape(64, 256))
        proj = dot(row_w, jnp.concatenate(cells, 0).astype(bf16), ((1,), (1,))).astype(bf16)
        row_pat[2 * n] = proj[:, :128]
        row_pat[2 * n + 1] = proj[:, 128:]
    loads[2].wait()
    col_w = col_w_in[...].T
    loads[3].wait()
    for n in range(9):
        cells = [jnp.broadcast_to(cols_in[q].astype(f32)[None], (16, 8, 256)).reshape(128, 256) for q in (2 * n, 2 * n + 1)]
        proj = dot(col_w, jnp.concatenate(cells, 0).astype(bf16), ((1,), (1,))).astype(bf16)
        col_pat[2 * n] = proj[:, :128]
        col_pat[2 * n + 1] = proj[:, 128:]
    loads[4].wait()
    for a in range(3):
        for b in range(3):
            taps[48 * b : 48 * b + 48, 48 * a : 48 * a + 48] = taps_in[a, b]
    loads[5].wait()
    loads[6].wait()

    lane = lax.broadcasted_iota(jnp.int32, (1, 128), 1)
    zero = jnp.zeros((), bf16)
    pair_w = pair_w_in[...]

    def pair_rows(p, carry):
        row = row_pat[p]
        tile_row = 32 * r + 16 * (lane // 64) + p - 1
        inside = ((tile_row >= 0) & (tile_row < 256)).astype(f32)
        first = inside * (c > 0).astype(f32)
        last = inside * (c < 15).astype(f32)
        at = pl.ds(pl.multiple_of(48 * p, 16), 48)
        for n in range(9):
            pair_act = jnp.concatenate(
                [jnp.maximum(row + col_pat[2 * n], zero), jnp.maximum(row + col_pat[2 * n + 1], zero)], axis=1
            )
            hidden = dot(pair_w, pair_act)
            keep = jnp.concatenate([first if n == 0 else inside, last if n == 8 else inside], axis=1)
            act[at, 256 * n : 256 * n + 256] = (jnp.maximum(hidden, 0.0) * keep).astype(bf16)
            base[at, 256 * n : 256 * n + 256] = hidden.astype(bf16)
        return carry

    lax.fori_loop(0, 18, pair_rows, 0)

    mix = mix_in[...]
    tap_w = taps[...]
    group = lane // 8

    def store(slot, e, m):
        return pltpu.make_async_copy(
            out_tile.at[slot, e], out_hbm.at[:, pl.ds(pl.multiple_of(128 * e + 16 * m, 16), 16), :], out_sem.at[slot, e]
        )

    def conv_rows(m, carry):
        slot = lax.rem(m, 2)
        mids = []
        for u in range(2):
            at = pl.ds(pl.multiple_of(96 * m + 48 * u, 16), 144)
            sums = dot(tap_w, act[at, :])
            mids.append(jnp.maximum(sums[:48, :2048] + sums[48:96, 128:2176] + sums[96:, 256:], 0.0).astype(bf16))
        mixed = [dot(mix, mids[u]) for u in range(2)]
        for u in range(2):
            here = base[pl.ds(pl.multiple_of(96 * m + 48 * u + 48, 16), 48), 128:2176]
            cells = (mixed[u] + here.astype(f32)).astype(bf16)
            tiles = [cells[:, 128 * q : 128 * q + 128] for q in range(16)]
            for d in (1, 2, 4, 8):
                stay = (group & d) == 0
                for q in range(16):
                    if q & d == 0:
                        x, y = tiles[q], tiles[q + d]
                        tiles[q] = jnp.where(stay, x, pltpu.roll(y, 8 * d, 1))
                        tiles[q + d] = jnp.where(stay, pltpu.roll(x, 128 - 8 * d, 1), y)
            for k in range(16):
                turn[k // 8, pl.ds(8 * u + k % 8, 48, stride=16), :] = tiles[k].astype(f32)

        @pl.when(m >= 2)
        def _():
            for e in range(2):
                store(slot, e, m - 2).wait()

        for e in range(2):
            out_tile[slot, e] = turn[e].reshape(48, 16, 128).astype(bf16)
            store(slot, e, m).start()
        return carry

    lax.fori_loop(0, 8, conv_rows, 0)
    for m in (6, 7):
        for e in range(2):
            store(m % 2, e, m).wait()


def block(rows, cols, row_weight, column_weight, pair_map_weight, dilated_weight, mixing_weight):
    hbm = pl.BlockSpec(memory_space=pltpu.HBM)
    return pl.pallas_call(
        block_kernel,
        out_shape=jax.ShapeDtypeStruct((48, 256, 128), bf16),
        in_specs=[hbm] * 7,
        out_specs=hbm,
        scratch_shapes=[
            pltpu.VMEM((34, 8, 256), bf16),
            pltpu.VMEM((18, 8, 256), bf16),
            pltpu.VMEM((256, 512), bf16),
            pltpu.VMEM((256, 512), bf16),
            pltpu.VMEM((48, 512), bf16),
            pltpu.VMEM((3, 3, 48, 48), bf16),
            pltpu.VMEM((48, 48), bf16),
            pltpu.VMEM((18, 512, 128), bf16),
            pltpu.VMEM((18, 512, 128), bf16),
            pltpu.VMEM((18 * 48, 18 * 128), bf16),
            pltpu.VMEM((18 * 48, 18 * 128), bf16),
            pltpu.VMEM((144, 144), bf16),
            pltpu.VMEM((2, 768, 128), f32),
            pltpu.VMEM((2, 2, 48, 16, 128), bf16),
            pltpu.SemaphoreType.DMA((7,)),
            pltpu.SemaphoreType.DMA((2, 2)),
        ],
        compiler_params=pltpu.CompilerParams(vmem_limit_bytes=(64 << 20) - (1 << 16)),
        name="pair_block",
    )(rows, cols, row_weight, column_weight, pair_map_weight.T, dilated_weight, mixing_weight)


def on_device(trunk, row_weight, column_weight, pair_map_weight, dilated_weight, mixing_weight):
    rows, cols = gather(trunk)
    return block(rows, cols, row_weight, column_weight, pair_map_weight, dilated_weight, mixing_weight)


def solution(mesh):
    return jax.shard_map(
        on_device,
        mesh=mesh,
        in_specs=(P(("row", "col"), None), P(), P(), P(), P(), P()),
        out_specs=P(None, "row", "col"),
        check_vma=False,
    )
```

```python
import jax
import jax.numpy as jnp
from jax import lax
from jax.experimental import pallas as pl
from jax.experimental.pallas import tpu as pltpu
from jax.sharding import PartitionSpec as P

bf16 = jnp.bfloat16
f32 = jnp.float32
MESH = pl.DeviceIdType.MESH
VMEM = pl.BlockSpec(memory_space=pltpu.VMEM)


def gather_kernel(x_ref, rows_ref, cols_ref, zero_ref, send_sem, rows_sem, cols_sem):
    r = lax.axis_index("row")
    c = lax.axis_index("col")
    k = lax.rem(c, 8)
    home = 2 * r + c // 8
    barrier = pltpu.get_barrier_semaphore()
    zero_ref[...] = jnp.zeros_like(zero_ref)

    def signal(row, col):
        pl.semaphore_signal(barrier, inc=1, device_id=(row, col), device_id_type=MESH)

    def each(count, body):
        def step(n, carry):
            body(n)
            return carry

        lax.fori_loop(0, count, step, 0)

    each(15, lambda n: signal(r, lax.rem(c + 1 + n, 16)))

    @pl.when(r > 0)
    def _():
        signal(r - 1, 15)

    @pl.when(r < 7)
    def _():
        signal(r + 1, 0)

    def signal_column_source(n):
        row, col = c // 2, 8 * lax.rem(c, 2) + n

        @pl.when((row != r) | (col != c))
        def _():
            signal(row, col)

    each(8, signal_column_source)

    @pl.when(c > 0)
    def _():
        row, col = (c - 1) // 2, 8 * lax.rem(c - 1, 2) + 7

        @pl.when((row != r) | (col != c))
        def _():
            signal(row, col)

    @pl.when(c < 15)
    def _():
        row, col = (c + 1) // 2, 8 * lax.rem(c + 1, 2)

        @pl.when((row != r) | (col != c))
        def _():
            signal(row, col)

    low_halo_rows = (c == 15) & (r < 7)
    high_halo_rows = (c == 0) & (r > 0)
    low_halo_cols = (k == 7) & (home < 15)
    high_halo_cols = (k == 0) & (home > 0)

    def away(col):
        return 7 + (col != c).astype(jnp.int32)

    peers = 15 + away(home)
    peers += 16 * (low_halo_rows | high_halo_rows).astype(jnp.int32)
    peers += low_halo_cols.astype(jnp.int32) * away(home + 1)
    peers += high_halo_cols.astype(jnp.int32) * away(home - 1)
    pl.semaphore_wait(barrier, peers)

    def remote(src, dst, sem, row, col):
        return pltpu.make_async_remote_copy(
            src_ref=src, dst_ref=dst, send_sem=send_sem, recv_sem=sem, device_id=(row, col), device_id_type=MESH
        )

    own_rows = rows_ref.at[pl.ds(1 + 2 * c, 2)]
    own_cols = cols_ref.at[pl.ds(1 + 2 * k, 2)]

    def to_column(src, dst, col):
        def body(n):
            row = lax.rem(r + n, 8)
            other = (row != r) | (col != c)

            @pl.when(other)
            def _():
                remote(src, dst, cols_sem, row, col).start()

            @pl.when(jnp.logical_not(other))
            def _():
                pltpu.make_async_copy(src, dst, cols_sem).start()

        each(8, body)

    @pl.when(low_halo_rows)
    def _():
        each(16, lambda n: remote(x_ref.at[1], rows_ref.at[0], rows_sem, r + 1, n).start())

    @pl.when(high_halo_rows)
    def _():
        each(16, lambda n: remote(x_ref.at[0], rows_ref.at[33], rows_sem, r - 1, n).start())

    @pl.when(low_halo_cols)
    def _():
        to_column(x_ref.at[1], cols_ref.at[0], home + 1)

    @pl.when(high_halo_cols)
    def _():
        to_column(x_ref.at[0], cols_ref.at[17], home - 1)

    to_column(x_ref, own_cols, home)
    each(15, lambda n: remote(x_ref, own_rows, rows_sem, r, lax.rem(c + 1 + n, 16)).start())
    pltpu.make_async_copy(x_ref, own_rows, rows_sem).start()

    @pl.when(r == 0)
    def _():
        pltpu.make_async_copy(zero_ref, rows_ref.at[0], rows_sem).start()

    @pl.when(r == 7)
    def _():
        pltpu.make_async_copy(zero_ref, rows_ref.at[33], rows_sem).start()

    @pl.when(c == 0)
    def _():
        pltpu.make_async_copy(zero_ref, cols_ref.at[0], cols_sem).start()

    @pl.when(c == 15)
    def _():
        pltpu.make_async_copy(zero_ref, cols_ref.at[17], cols_sem).start()

    def sent(blocks):
        part = rows_ref.at[pl.ds(0, blocks)]
        pltpu.make_async_copy(part, part, send_sem).wait()

    sent(30)

    sent(14)

    @pl.when(home != c)
    def _():
        sent(2)

    @pl.when(low_halo_rows)
    def _():
        sent(16)

    @pl.when(high_halo_rows)
    def _():
        sent(16)

    def column_sent(col):
        sent(7)

        @pl.when(col != c)
        def _():
            sent(1)

    @pl.when(low_halo_cols)
    def _():
        column_sent(home + 1)

    @pl.when(high_halo_cols)
    def _():
        column_sent(home - 1)

    pltpu.make_async_copy(rows_ref, rows_ref, rows_sem).wait()
    pltpu.make_async_copy(cols_ref, cols_ref, cols_sem).wait()


def gather(trunk):
    width = trunk.shape[1]
    return pl.pallas_call(
        gather_kernel,
        out_shape=(
            jax.ShapeDtypeStruct((34, 8, width), bf16),
            jax.ShapeDtypeStruct((18, 8, width), bf16),
        ),
        in_specs=[VMEM],
        out_specs=(VMEM, VMEM),
        scratch_shapes=[
            pltpu.VMEM((8, width), bf16),
            pltpu.SemaphoreType.DMA,
            pltpu.SemaphoreType.DMA,
            pltpu.SemaphoreType.DMA,
        ],
        compiler_params=pltpu.CompilerParams(collective_id=0, has_side_effects=True),
        name="gather_bins",
    )(trunk.reshape(2, 8, width))


def dot(a, b, dims=((1,), (0,))):
    return lax.dot_general(a, b, (dims, ((), ())), preferred_element_type=f32)


def block_kernel(
    rows_hbm, cols_hbm, row_w_hbm, col_w_hbm, pair_w_hbm, taps_hbm, mix_hbm, out_hbm,
    rows_in, cols_in, row_w_in, col_w_in, pair_w_in, taps_in, mix_in,
    row_pat, col_pat, act, base, taps, turn, held, out_tile, in_sem, out_sem,
):
    r = lax.axis_index("row")
    c = lax.axis_index("col")
    loads = [
        pltpu.make_async_copy(src, dst, in_sem.at[n])
        for n, (src, dst) in enumerate(
            (
                (row_w_hbm, row_w_in),
                (rows_hbm, rows_in),
                (col_w_hbm, col_w_in),
                (cols_hbm, cols_in),
                (taps_hbm, taps_in),
                (pair_w_hbm, pair_w_in),
                (mix_hbm, mix_in),
            )
        )
    ]
    for load in loads:
        load.start()

    loads[0].wait()
    row_w = row_w_in[...].T
    loads[1].wait()
    for n in range(9):
        cells = []
        for p in (2 * n, 2 * n + 1):
            for e in range(2):
                bins = rows_in[16 * e + p].astype(f32)
                cells.append(jnp.broadcast_to(bins[:, None, :], (8, 8, 256)).reshape(64, 256))
        proj = dot(row_w, jnp.concatenate(cells, 0).astype(bf16), ((1,), (1,))).astype(bf16)
        row_pat[2 * n] = proj[:, :128]
        row_pat[2 * n + 1] = proj[:, 128:]
    loads[2].wait()
    col_w = col_w_in[...].T
    loads[3].wait()
    for n in range(9):
        cells = [jnp.broadcast_to(cols_in[q].astype(f32)[None], (16, 8, 256)).reshape(128, 256) for q in (2 * n, 2 * n + 1)]
        proj = dot(col_w, jnp.concatenate(cells, 0).astype(bf16), ((1,), (1,))).astype(bf16)
        col_pat[2 * n] = proj[:, :128]
        col_pat[2 * n + 1] = proj[:, 128:]
    loads[4].wait()
    for a in range(3):
        for b in range(3):
            taps[48 * b : 48 * b + 48, 48 * a : 48 * a + 48] = taps_in[a, b]
    loads[5].wait()
    loads[6].wait()

    lane = lax.broadcasted_iota(jnp.int32, (1, 128), 1)
    zero = jnp.zeros((), bf16)
    pair_w = pair_w_in[...]

    def pair_rows(p, carry):
        row = row_pat[p]
        tile_row = 32 * r + 16 * (lane // 64) + p - 1
        inside = ((tile_row >= 0) & (tile_row < 256)).astype(f32)
        first = inside * (c > 0).astype(f32)
        last = inside * (c < 15).astype(f32)
        at = pl.ds(pl.multiple_of(48 * p, 16), 48)
        for n in range(9):
            pair_act = jnp.concatenate(
                [jnp.maximum(row + col_pat[2 * n], zero), jnp.maximum(row + col_pat[2 * n + 1], zero)], axis=1
            )
            hidden = dot(pair_w, pair_act)
            keep = jnp.concatenate([first if n == 0 else inside, last if n == 8 else inside], axis=1)
            act[at, 256 * n : 256 * n + 256] = (jnp.maximum(hidden, 0.0) * keep).astype(bf16)
            base[at, 256 * n : 256 * n + 256] = hidden.astype(bf16)
        return carry

    lax.fori_loop(0, 18, pair_rows, 0, unroll=6)

    mix = mix_in[...]
    tap_w = taps[...]
    group = lane // 8

    def store(slot, e, m):
        return pltpu.make_async_copy(
            out_tile.at[slot, e], out_hbm.at[:, pl.ds(pl.multiple_of(128 * e + 16 * m, 16), 16), :], out_sem.at[slot, e]
        )

    def conv_rows(m):
        mids = []
        for u in range(2):
            at = pl.ds(pl.multiple_of(96 * m + 48 * u, 16), 144)
            sums = dot(tap_w, act[at, :])
            mids.append(jnp.maximum(sums[:48, :2048] + sums[48:96, 128:2176] + sums[96:, 256:], 0.0).astype(bf16))
        mixed = [dot(mix, mids[u]) for u in range(2)]
        for u in range(2):
            here = base[pl.ds(pl.multiple_of(96 * m + 48 * u + 48, 16), 48), 128:2176]
            held[u] = (mixed[u] + here.astype(f32)).astype(bf16)

    def turn_rows(m):
        for u in range(2):
            tiles = [held[u, :, 128 * q : 128 * q + 128] for q in range(16)]
            tiles = [pltpu.roll(tile, 8 * q, 1) if q else tile for q, tile in enumerate(tiles)]
            tiles = [tiles[-k % 16] for k in range(16)]
            for d in (1, 2, 4, 8):
                move = (group & d) != 0
                tiles = [jnp.where(move, tiles[(k - d) % 16], tiles[k]) for k in range(16)]
            tiles = [pltpu.roll(tile, 128 - 8 * k, 1) if k else tile for k, tile in enumerate(tiles)]
            for k in range(16):
                turn[k // 8, u, pl.ds(k % 8, 48, stride=9), :] = tiles[k].astype(f32)

    def put_rows(m):
        slot = lax.rem(m, 2)

        @pl.when(m >= 2)
        def _():
            for e in range(2):
                store(slot, e, m - 2).wait()

        for e in range(2):
            halves = [jnp.stack([turn[e, u, 9 * o : 9 * o + 8] for o in range(48)]) for u in range(2)]
            out_tile[slot, e] = jnp.concatenate(halves, axis=1).astype(bf16)
            store(slot, e, m).start()

    def step(m, carry):
        turn_rows(m - 1)
        conv_rows(m)
        put_rows(m - 1)
        return carry

    conv_rows(0)
    lax.fori_loop(1, 8, step, 0)
    turn_rows(7)
    put_rows(jnp.int32(7))
    for m in (6, 7):
        for e in range(2):
            store(m % 2, e, m).wait()


def block(rows, cols, row_weight, column_weight, pair_map_weight, dilated_weight, mixing_weight):
    hbm = pl.BlockSpec(memory_space=pltpu.HBM)
    return pl.pallas_call(
        block_kernel,
        out_shape=jax.ShapeDtypeStruct((48, 256, 128), bf16),
        in_specs=[hbm] * 7,
        out_specs=hbm,
        scratch_shapes=[
            pltpu.VMEM((34, 8, 256), bf16),
            pltpu.VMEM((18, 8, 256), bf16),
            pltpu.VMEM((256, 512), bf16),
            pltpu.VMEM((256, 512), bf16),
            pltpu.VMEM((48, 512), bf16),
            pltpu.VMEM((3, 3, 48, 48), bf16),
            pltpu.VMEM((48, 48), bf16),
            pltpu.VMEM((18, 512, 128), bf16),
            pltpu.VMEM((18, 512, 128), bf16),
            pltpu.VMEM((18 * 48, 18 * 128), bf16),
            pltpu.VMEM((18 * 48, 18 * 128), bf16),
            pltpu.VMEM((144, 144), bf16),
            pltpu.VMEM((2, 2, 432, 128), f32),
            pltpu.VMEM((2, 48, 2048), bf16),
            pltpu.VMEM((2, 2, 48, 16, 128), bf16),
            pltpu.SemaphoreType.DMA((7,)),
            pltpu.SemaphoreType.DMA((2, 2)),
        ],
        compiler_params=pltpu.CompilerParams(vmem_limit_bytes=(64 << 20) - (1 << 16)),
        name="pair_block",
    )(rows, cols, row_weight, column_weight, pair_map_weight.T, dilated_weight, mixing_weight)


def on_device(trunk, row_weight, column_weight, pair_map_weight, dilated_weight, mixing_weight):
    rows, cols = gather(trunk)
    return block(rows, cols, row_weight, column_weight, pair_map_weight, dilated_weight, mixing_weight)


def solution(mesh):
    return jax.shard_map(
        on_device,
        mesh=mesh,
        in_specs=(P(("row", "col"), None), P(), P(), P(), P(), P()),
        out_specs=P(None, "row", "col"),
        check_vma=False,
    )
```

```python
import jax
import jax.numpy as jnp
from jax import lax
from jax.experimental import pallas as pl
from jax.experimental.pallas import tpu as pltpu
from jax.sharding import PartitionSpec as P

bf16 = jnp.bfloat16
f32 = jnp.float32
MESH = pl.DeviceIdType.MESH
VMEM = pl.BlockSpec(memory_space=pltpu.VMEM)


def gather_kernel(x_ref, rows_ref, cols_ref, zero_ref, send_sem, rows_sem, cols_sem):
    r = lax.axis_index("row")
    c = lax.axis_index("col")
    k = lax.rem(c, 8)
    home = 2 * r + c // 8
    barrier = pltpu.get_barrier_semaphore()
    zero_ref[...] = jnp.zeros_like(zero_ref)

    def signal(row, col):
        pl.semaphore_signal(barrier, inc=1, device_id=(row, col), device_id_type=MESH)

    def each(count, body):
        def step(n, carry):
            body(n)
            return carry

        lax.fori_loop(0, count, step, 0)

    each(15, lambda n: signal(r, lax.rem(c + 1 + n, 16)))

    @pl.when(r > 0)
    def _():
        signal(r - 1, 15)

    @pl.when(r < 7)
    def _():
        signal(r + 1, 0)

    def signal_column_source(n):
        row, col = c // 2, 8 * lax.rem(c, 2) + n

        @pl.when((row != r) | (col != c))
        def _():
            signal(row, col)

    each(8, signal_column_source)

    @pl.when(c > 0)
    def _():
        row, col = (c - 1) // 2, 8 * lax.rem(c - 1, 2) + 7

        @pl.when((row != r) | (col != c))
        def _():
            signal(row, col)

    @pl.when(c < 15)
    def _():
        row, col = (c + 1) // 2, 8 * lax.rem(c + 1, 2)

        @pl.when((row != r) | (col != c))
        def _():
            signal(row, col)

    low_halo_rows = (c == 15) & (r < 7)
    high_halo_rows = (c == 0) & (r > 0)
    low_halo_cols = (k == 7) & (home < 15)
    high_halo_cols = (k == 0) & (home > 0)

    def away(col):
        return 7 + (col != c).astype(jnp.int32)

    peers = 15 + away(home)
    peers += 16 * (low_halo_rows | high_halo_rows).astype(jnp.int32)
    peers += low_halo_cols.astype(jnp.int32) * away(home + 1)
    peers += high_halo_cols.astype(jnp.int32) * away(home - 1)
    pl.semaphore_wait(barrier, peers)

    def remote(src, dst, sem, row, col):
        return pltpu.make_async_remote_copy(
            src_ref=src, dst_ref=dst, send_sem=send_sem, recv_sem=sem, device_id=(row, col), device_id_type=MESH
        )

    own_rows = rows_ref.at[pl.ds(1 + 2 * c, 2)]
    own_cols = cols_ref.at[pl.ds(1 + 2 * k, 2)]

    def to_column(src, dst, col):
        def body(n):
            row = lax.rem(r + n, 8)
            other = (row != r) | (col != c)

            @pl.when(other)
            def _():
                remote(src, dst, cols_sem, row, col).start()

            @pl.when(jnp.logical_not(other))
            def _():
                pltpu.make_async_copy(src, dst, cols_sem).start()

        each(8, body)

    @pl.when(low_halo_rows)
    def _():
        each(16, lambda n: remote(x_ref.at[1], rows_ref.at[0], rows_sem, r + 1, n).start())

    @pl.when(high_halo_rows)
    def _():
        each(16, lambda n: remote(x_ref.at[0], rows_ref.at[33], rows_sem, r - 1, n).start())

    @pl.when(low_halo_cols)
    def _():
        to_column(x_ref.at[1], cols_ref.at[0], home + 1)

    @pl.when(high_halo_cols)
    def _():
        to_column(x_ref.at[0], cols_ref.at[17], home - 1)

    to_column(x_ref, own_cols, home)
    each(15, lambda n: remote(x_ref, own_rows, rows_sem, r, lax.rem(c + 1 + n, 16)).start())
    pltpu.make_async_copy(x_ref, own_rows, rows_sem).start()

    @pl.when(r == 0)
    def _():
        pltpu.make_async_copy(zero_ref, rows_ref.at[0], rows_sem).start()

    @pl.when(r == 7)
    def _():
        pltpu.make_async_copy(zero_ref, rows_ref.at[33], rows_sem).start()

    @pl.when(c == 0)
    def _():
        pltpu.make_async_copy(zero_ref, cols_ref.at[0], cols_sem).start()

    @pl.when(c == 15)
    def _():
        pltpu.make_async_copy(zero_ref, cols_ref.at[17], cols_sem).start()

    def sent(blocks):
        part = rows_ref.at[pl.ds(0, blocks)]
        pltpu.make_async_copy(part, part, send_sem).wait()

    sent(30)

    sent(14)

    @pl.when(home != c)
    def _():
        sent(2)

    @pl.when(low_halo_rows)
    def _():
        sent(16)

    @pl.when(high_halo_rows)
    def _():
        sent(16)

    def column_sent(col):
        sent(7)

        @pl.when(col != c)
        def _():
            sent(1)

    @pl.when(low_halo_cols)
    def _():
        column_sent(home + 1)

    @pl.when(high_halo_cols)
    def _():
        column_sent(home - 1)

    pltpu.make_async_copy(rows_ref, rows_ref, rows_sem).wait()
    pltpu.make_async_copy(cols_ref, cols_ref, cols_sem).wait()


def gather(trunk):
    width = trunk.shape[1]
    return pl.pallas_call(
        gather_kernel,
        out_shape=(
            jax.ShapeDtypeStruct((34, 8, width), bf16),
            jax.ShapeDtypeStruct((18, 8, width), bf16),
        ),
        in_specs=[VMEM],
        out_specs=(pl.BlockSpec(memory_space=pltpu.HBM),) * 2,
        scratch_shapes=[
            pltpu.VMEM((8, width), bf16),
            pltpu.SemaphoreType.DMA,
            pltpu.SemaphoreType.DMA,
            pltpu.SemaphoreType.DMA,
        ],
        compiler_params=pltpu.CompilerParams(collective_id=0, has_side_effects=True),
        name="gather_bins",
    )(trunk.reshape(2, 8, width))


def dot(a, b, dims=((1,), (0,))):
    return lax.dot_general(a, b, (dims, ((), ())), preferred_element_type=f32)


def block_kernel(
    rows_hbm, cols_hbm, row_w_hbm, col_w_hbm, pair_w_hbm, taps_hbm, mix_hbm, out_hbm,
    rows_in, cols_in, row_w_in, col_w_in, pair_w_in, taps_in, mix_in,
    row_pat, col_pat, act, base, taps, turn, held, out_tile, in_sem, out_sem,
):
    r = lax.axis_index("row")
    c = lax.axis_index("col")
    loads = [
        pltpu.make_async_copy(src, dst, in_sem.at[n])
        for n, (src, dst) in enumerate(
            (
                (row_w_hbm, row_w_in),
                (rows_hbm, rows_in),
                (col_w_hbm, col_w_in),
                (cols_hbm, cols_in),
                (taps_hbm, taps_in),
                (pair_w_hbm, pair_w_in),
                (mix_hbm, mix_in),
            )
        )
    ]
    for load in loads:
        load.start()

    loads[0].wait()
    row_w = row_w_in[...].T
    loads[1].wait()
    for n in range(9):
        cells = []
        for p in (2 * n, 2 * n + 1):
            for e in range(2):
                bins = rows_in[16 * e + p].astype(f32)
                cells.append(jnp.broadcast_to(bins[:, None, :], (8, 8, 256)).reshape(64, 256))
        proj = dot(row_w, jnp.concatenate(cells, 0).astype(bf16), ((1,), (1,))).astype(bf16)
        row_pat[2 * n] = proj[:, :128]
        row_pat[2 * n + 1] = proj[:, 128:]
    loads[2].wait()
    col_w = col_w_in[...].T
    loads[3].wait()
    for n in range(9):
        cells = [jnp.broadcast_to(cols_in[q].astype(f32)[None], (16, 8, 256)).reshape(128, 256) for q in (2 * n, 2 * n + 1)]
        proj = dot(col_w, jnp.concatenate(cells, 0).astype(bf16), ((1,), (1,))).astype(bf16)
        col_pat[2 * n] = proj[:, :128]
        col_pat[2 * n + 1] = proj[:, 128:]
    loads[4].wait()
    for a in range(3):
        for b in range(3):
            taps[48 * b : 48 * b + 48, 48 * a : 48 * a + 48] = taps_in[a, b]
    loads[5].wait()
    loads[6].wait()

    lane = lax.broadcasted_iota(jnp.int32, (1, 128), 1)
    zero = jnp.zeros((), bf16)
    pair_w = pair_w_in[...]

    def pair_rows(p, carry):
        row = row_pat[p]
        tile_row = 32 * r + 16 * (lane // 64) + p - 1
        inside = ((tile_row >= 0) & (tile_row < 256)).astype(f32)
        first = inside * (c > 0).astype(f32)
        last = inside * (c < 15).astype(f32)
        at = pl.ds(pl.multiple_of(48 * p, 16), 48)
        for n in range(9):
            pair_act = jnp.concatenate(
                [jnp.maximum(row + col_pat[2 * n], zero), jnp.maximum(row + col_pat[2 * n + 1], zero)], axis=1
            )
            hidden = dot(pair_w, pair_act)
            keep = jnp.concatenate([first if n == 0 else inside, last if n == 8 else inside], axis=1)
            act[at, 256 * n : 256 * n + 256] = (jnp.maximum(hidden, 0.0) * keep).astype(bf16)
            base[at, 256 * n : 256 * n + 256] = hidden.astype(bf16)
        return carry

    lax.fori_loop(0, 18, pair_rows, 0, unroll=18)

    mix = mix_in[...]
    tap_w = taps[...]
    group = lane // 8

    def store(slot, e, m):
        return pltpu.make_async_copy(
            out_tile.at[slot, e], out_hbm.at[:, pl.ds(pl.multiple_of(128 * e + 16 * m, 16), 16), :], out_sem.at[slot, e]
        )

    def conv_rows(m):
        mids = []
        for u in range(2):
            at = pl.ds(pl.multiple_of(96 * m + 48 * u, 16), 144)
            sums = dot(tap_w, act[at, :])
            mids.append(jnp.maximum(sums[:48, :2048] + sums[48:96, 128:2176] + sums[96:, 256:], 0.0).astype(bf16))
        mixed = [dot(mix, mids[u]) for u in range(2)]
        for u in range(2):
            here = base[pl.ds(pl.multiple_of(96 * m + 48 * u + 48, 16), 48), 128:2176]
            held[u] = (mixed[u] + here.astype(f32)).astype(bf16)

    def turn_rows(m):
        for u in range(2):
            tiles = [held[u, :, 128 * q : 128 * q + 128] for q in range(16)]
            tiles = [pltpu.roll(tile, 8 * q, 1) if q else tile for q, tile in enumerate(tiles)]
            tiles = [tiles[-k % 16] for k in range(16)]
            for d in (1, 2, 4, 8):
                move = (group & d) != 0
                tiles = [jnp.where(move, tiles[(k - d) % 16], tiles[k]) for k in range(16)]
            tiles = [pltpu.roll(tile, 128 - 8 * k, 1) if k else tile for k, tile in enumerate(tiles)]
            for k in range(16):
                turn[k // 8, u, pl.ds(k % 8, 48, stride=9), :] = tiles[k].astype(f32)

    def put_rows(m):
        slot = lax.rem(m, 2)

        @pl.when(m >= 2)
        def _():
            for e in range(2):
                store(slot, e, m - 2).wait()

        for e in range(2):
            halves = [jnp.stack([turn[e, u, 9 * o : 9 * o + 8] for o in range(48)]) for u in range(2)]
            out_tile[slot, e] = jnp.concatenate(halves, axis=1).astype(bf16)
            store(slot, e, m).start()

    def step(m, carry):
        turn_rows(m - 1)
        conv_rows(m)
        put_rows(m - 1)
        return carry

    conv_rows(0)
    lax.fori_loop(1, 8, step, 0)
    turn_rows(7)
    put_rows(jnp.int32(7))
    for m in (6, 7):
        for e in range(2):
            store(m % 2, e, m).wait()


def block(rows, cols, row_weight, column_weight, pair_map_weight, dilated_weight, mixing_weight):
    hbm = pl.BlockSpec(memory_space=pltpu.HBM)
    return pl.pallas_call(
        block_kernel,
        out_shape=jax.ShapeDtypeStruct((48, 256, 128), bf16),
        in_specs=[hbm] * 7,
        out_specs=hbm,
        scratch_shapes=[
            pltpu.VMEM((34, 8, 256), bf16),
            pltpu.VMEM((18, 8, 256), bf16),
            pltpu.VMEM((256, 512), bf16),
            pltpu.VMEM((256, 512), bf16),
            pltpu.VMEM((48, 512), bf16),
            pltpu.VMEM((3, 3, 48, 48), bf16),
            pltpu.VMEM((48, 48), bf16),
            pltpu.VMEM((18, 512, 128), bf16),
            pltpu.VMEM((18, 512, 128), bf16),
            pltpu.VMEM((18 * 48, 18 * 128), bf16),
            pltpu.VMEM((18 * 48, 18 * 128), bf16),
            pltpu.VMEM((144, 144), bf16),
            pltpu.VMEM((2, 2, 432, 128), f32),
            pltpu.VMEM((2, 48, 2048), bf16),
            pltpu.VMEM((2, 2, 48, 16, 128), bf16),
            pltpu.SemaphoreType.DMA((7,)),
            pltpu.SemaphoreType.DMA((2, 2)),
        ],
        compiler_params=pltpu.CompilerParams(vmem_limit_bytes=(64 << 20) - (1 << 16)),
        name="pair_block",
    )(rows, cols, row_weight, column_weight, pair_map_weight.T, dilated_weight, mixing_weight)


def on_device(trunk, row_weight, column_weight, pair_map_weight, dilated_weight, mixing_weight):
    rows, cols = gather(trunk)
    return block(rows, cols, row_weight, column_weight, pair_map_weight, dilated_weight, mixing_weight)


def solution(mesh):
    return jax.shard_map(
        on_device,
        mesh=mesh,
        in_specs=(P(("row", "col"), None), P(), P(), P(), P(), P()),
        out_specs=P(None, "row", "col"),
        check_vma=False,
    )
```

```python
import jax
import jax.numpy as jnp
from jax import lax
from jax.experimental import pallas as pl
from jax.experimental.pallas import tpu as pltpu
from jax.sharding import PartitionSpec as P

bf16 = jnp.bfloat16
f32 = jnp.float32
MESH = pl.DeviceIdType.MESH
VMEM = pl.BlockSpec(memory_space=pltpu.VMEM)


def gather_kernel(x_ref, rows_ref, cols_ref, zero_ref, send_sem, rows_sem, cols_sem):
    r = lax.axis_index("row")
    c = lax.axis_index("col")
    k = lax.rem(c, 8)
    home = 2 * r + c // 8
    barrier = pltpu.get_barrier_semaphore()
    zero_ref[...] = jnp.zeros_like(zero_ref)

    def signal(row, col):
        pl.semaphore_signal(barrier, inc=1, device_id=(row, col), device_id_type=MESH)

    def each(count, body):
        def step(n, carry):
            body(n)
            return carry

        lax.fori_loop(0, count, step, 0)

    each(15, lambda n: signal(r, lax.rem(c + 1 + n, 16)))

    @pl.when(r > 0)
    def _():
        signal(r - 1, 15)

    @pl.when(r < 7)
    def _():
        signal(r + 1, 0)

    def signal_column_source(n):
        row, col = c // 2, 8 * lax.rem(c, 2) + n

        @pl.when((row != r) | (col != c))
        def _():
            signal(row, col)

    each(8, signal_column_source)

    @pl.when(c > 0)
    def _():
        row, col = (c - 1) // 2, 8 * lax.rem(c - 1, 2) + 7

        @pl.when((row != r) | (col != c))
        def _():
            signal(row, col)

    @pl.when(c < 15)
    def _():
        row, col = (c + 1) // 2, 8 * lax.rem(c + 1, 2)

        @pl.when((row != r) | (col != c))
        def _():
            signal(row, col)

    low_halo_rows = (c == 15) & (r < 7)
    high_halo_rows = (c == 0) & (r > 0)
    low_halo_cols = (k == 7) & (home < 15)
    high_halo_cols = (k == 0) & (home > 0)

    def away(col):
        return 7 + (col != c).astype(jnp.int32)

    peers = 15 + away(home)
    peers += 16 * (low_halo_rows | high_halo_rows).astype(jnp.int32)
    peers += low_halo_cols.astype(jnp.int32) * away(home + 1)
    peers += high_halo_cols.astype(jnp.int32) * away(home - 1)
    pl.semaphore_wait(barrier, peers)

    def remote(src, dst, sem, row, col):
        return pltpu.make_async_remote_copy(
            src_ref=src, dst_ref=dst, send_sem=send_sem, recv_sem=sem, device_id=(row, col), device_id_type=MESH
        )

    own_rows = rows_ref.at[pl.ds(1 + 2 * c, 2)]
    own_cols = cols_ref.at[pl.ds(1 + 2 * k, 2)]

    def to_column(src, dst, col):
        def body(n):
            row = lax.rem(r + n, 8)
            other = (row != r) | (col != c)

            @pl.when(other)
            def _():
                remote(src, dst, cols_sem, row, col).start()

            @pl.when(jnp.logical_not(other))
            def _():
                pltpu.make_async_copy(src, dst, cols_sem).start()

        each(8, body)

    @pl.when(low_halo_rows)
    def _():
        each(16, lambda n: remote(x_ref.at[1], rows_ref.at[0], rows_sem, r + 1, n).start())

    @pl.when(high_halo_rows)
    def _():
        each(16, lambda n: remote(x_ref.at[0], rows_ref.at[33], rows_sem, r - 1, n).start())

    @pl.when(low_halo_cols)
    def _():
        to_column(x_ref.at[1], cols_ref.at[0], home + 1)

    @pl.when(high_halo_cols)
    def _():
        to_column(x_ref.at[0], cols_ref.at[17], home - 1)

    to_column(x_ref, own_cols, home)
    each(15, lambda n: remote(x_ref, own_rows, rows_sem, r, lax.rem(c + 1 + n, 16)).start())
    pltpu.make_async_copy(x_ref, own_rows, rows_sem).start()

    @pl.when(r == 0)
    def _():
        pltpu.make_async_copy(zero_ref, rows_ref.at[0], rows_sem).start()

    @pl.when(r == 7)
    def _():
        pltpu.make_async_copy(zero_ref, rows_ref.at[33], rows_sem).start()

    @pl.when(c == 0)
    def _():
        pltpu.make_async_copy(zero_ref, cols_ref.at[0], cols_sem).start()

    @pl.when(c == 15)
    def _():
        pltpu.make_async_copy(zero_ref, cols_ref.at[17], cols_sem).start()

    def sent(blocks):
        part = rows_ref.at[pl.ds(0, blocks)]
        pltpu.make_async_copy(part, part, send_sem).wait()

    sent(30)

    sent(14)

    @pl.when(home != c)
    def _():
        sent(2)

    @pl.when(low_halo_rows)
    def _():
        sent(16)

    @pl.when(high_halo_rows)
    def _():
        sent(16)

    def column_sent(col):
        sent(7)

        @pl.when(col != c)
        def _():
            sent(1)

    @pl.when(low_halo_cols)
    def _():
        column_sent(home + 1)

    @pl.when(high_halo_cols)
    def _():
        column_sent(home - 1)

    pltpu.make_async_copy(rows_ref, rows_ref, rows_sem).wait()
    pltpu.make_async_copy(cols_ref, cols_ref, cols_sem).wait()


def gather(trunk):
    width = trunk.shape[1]
    return pl.pallas_call(
        gather_kernel,
        out_shape=(
            jax.ShapeDtypeStruct((34, 8, width), bf16),
            jax.ShapeDtypeStruct((18, 8, width), bf16),
        ),
        in_specs=[VMEM],
        out_specs=(pl.BlockSpec(memory_space=pltpu.HBM),) * 2,
        scratch_shapes=[
            pltpu.VMEM((8, width), bf16),
            pltpu.SemaphoreType.DMA,
            pltpu.SemaphoreType.DMA,
            pltpu.SemaphoreType.DMA,
        ],
        compiler_params=pltpu.CompilerParams(collective_id=0, has_side_effects=True),
        name="gather_bins",
    )(trunk.reshape(2, 8, width))


def dot(a, b, dims=((1,), (0,))):
    return lax.dot_general(a, b, (dims, ((), ())), preferred_element_type=f32)


def block_kernel(
    rows_hbm, cols_hbm, row_w_hbm, col_w_hbm, pair_w_hbm, taps_hbm, mix_hbm, out_hbm,
    rows_in, cols_in, row_w_in, col_w_in, pair_w_in, taps_in, mix_in,
    row_pat, col_pat, act, base, taps, turn, held, out_tile, in_sem, out_sem,
):
    r = lax.axis_index("row")
    c = lax.axis_index("col")
    loads = [
        pltpu.make_async_copy(src, dst, in_sem.at[n])
        for n, (src, dst) in enumerate(
            (
                (row_w_hbm, row_w_in),
                (rows_hbm, rows_in),
                (col_w_hbm, col_w_in),
                (cols_hbm, cols_in),
                (taps_hbm, taps_in),
                (pair_w_hbm, pair_w_in),
                (mix_hbm, mix_in),
            )
        )
    ]
    for load in loads:
        load.start()

    loads[0].wait()
    row_w = row_w_in[...].T
    loads[1].wait()
    for n in range(9):
        cells = []
        for p in (2 * n, 2 * n + 1)[: 1 if n == 8 else 2]:
            for e in range(2):
                bins = rows_in[33 * e if p == 16 else 16 * e + p + 1].astype(f32)
                cells.append(jnp.broadcast_to(bins[:, None, :], (8, 8, 256)).reshape(64, 256))
        proj = dot(row_w, jnp.concatenate(cells, 0).astype(bf16), ((1,), (1,))).astype(bf16)
        row_pat[2 * n] = proj[:, :128]
        if n < 8:
            row_pat[2 * n + 1] = proj[:, 128:]
    loads[2].wait()
    col_w = col_w_in[...].T
    loads[3].wait()
    for n in range(9):
        cells = [jnp.broadcast_to(cols_in[q].astype(f32)[None], (16, 8, 256)).reshape(128, 256) for q in (2 * n, 2 * n + 1)]
        proj = dot(col_w, jnp.concatenate(cells, 0).astype(bf16), ((1,), (1,))).astype(bf16)
        col_pat[2 * n] = proj[:, :128]
        col_pat[2 * n + 1] = proj[:, 128:]
    loads[4].wait()
    for a in range(3):
        for b in range(3):
            taps[48 * b : 48 * b + 48, 48 * a : 48 * a + 48] = taps_in[a, b]
    loads[5].wait()
    loads[6].wait()

    lane = lax.broadcasted_iota(jnp.int32, (1, 128), 1)
    zero = jnp.zeros((), bf16)
    pair_w = pair_w_in[...]

    not_first = (c > 0).astype(f32)
    not_last = (c < 15).astype(f32)
    left = lane < 64

    def pair_chunk(row, n):
        pair_act = jnp.concatenate(
            [jnp.maximum(row + col_pat[2 * n], zero), jnp.maximum(row + col_pat[2 * n + 1], zero)], axis=1
        )
        hidden = dot(pair_w, pair_act)
        shown = jnp.maximum(hidden, 0.0)
        if n == 0:
            shown = jnp.concatenate([shown[:, :128] * not_first, shown[:, 128:]], axis=1)
        if n == 8:
            shown = jnp.concatenate([shown[:, :128], shown[:, 128:] * not_last], axis=1)
        return hidden, shown

    def pair_rows(p, carry):
        row = row_pat[p]
        at = pl.ds(pl.multiple_of(48 * p + 48, 16), 48)
        for n in range(9):
            hidden, shown = pair_chunk(row, n)
            act[at, 256 * n : 256 * n + 256] = shown.astype(bf16)
            base[at, 256 * n : 256 * n + 256] = hidden.astype(bf16)
        return carry

    lax.fori_loop(0, 16, pair_rows, 0, unroll=16)

    inside = jnp.where(left, (r > 0).astype(f32), (r < 7).astype(f32))
    inside = jnp.concatenate([inside, inside], axis=1)
    halo_row = row_pat[16]
    for n in range(9):
        halo = (pair_chunk(halo_row, n)[1] * inside).astype(bf16)
        for u in range(2):
            at = slice(256 * n + 128 * u, 256 * n + 128 * u + 128)
            outer = halo[:, 128 * u : 128 * u + 128]
            act[0:48, at] = jnp.where(left, outer, pltpu.roll(act[768:816, at], 64, 1))
            act[816:864, at] = jnp.where(left, pltpu.roll(act[48:96, at], 64, 1), outer)

    mix = mix_in[...]
    tap_w = taps[...]
    group = lane // 8

    def store(slot, e, m):
        return pltpu.make_async_copy(
            out_tile.at[slot, e], out_hbm.at[:, pl.ds(pl.multiple_of(128 * e + 16 * m, 16), 16), :], out_sem.at[slot, e]
        )

    def conv_rows(m):
        mids = []
        for u in range(2):
            at = pl.ds(pl.multiple_of(96 * m + 48 * u, 16), 144)
            sums = dot(tap_w, act[at, :])
            mids.append(jnp.maximum(sums[:48, :2048] + sums[48:96, 128:2176] + sums[96:, 256:], 0.0).astype(bf16))
        mixed = [dot(mix, mids[u]) for u in range(2)]
        for u in range(2):
            here = base[pl.ds(pl.multiple_of(96 * m + 48 * u + 48, 16), 48), 128:2176]
            held[u] = (mixed[u] + here.astype(f32)).astype(bf16)

    def turn_rows(m):
        for u in range(2):
            tiles = [held[u, :, 128 * q : 128 * q + 128] for q in range(16)]
            tiles = [pltpu.roll(tile, 8 * q, 1) if q else tile for q, tile in enumerate(tiles)]
            tiles = [tiles[-k % 16] for k in range(16)]
            for d in (1, 2, 4, 8):
                move = (group & d) != 0
                tiles = [jnp.where(move, tiles[(k - d) % 16], tiles[k]) for k in range(16)]
            tiles = [pltpu.roll(tile, 128 - 8 * k, 1) if k else tile for k, tile in enumerate(tiles)]
            for k in range(16):
                turn[k // 8, u, pl.ds(k % 8, 48, stride=9), :] = tiles[k].astype(f32)

    def put_rows(m):
        slot = lax.rem(m, 2)

        @pl.when(m >= 2)
        def _():
            for e in range(2):
                store(slot, e, m - 2).wait()

        for e in range(2):
            halves = [jnp.stack([turn[e, u, 9 * o : 9 * o + 8] for o in range(48)]) for u in range(2)]
            out_tile[slot, e] = jnp.concatenate(halves, axis=1).astype(bf16)
            store(slot, e, m).start()

    def step(m, carry):
        turn_rows(m - 1)
        conv_rows(m)
        put_rows(m - 1)
        return carry

    conv_rows(0)
    lax.fori_loop(1, 8, step, 0)
    turn_rows(7)
    put_rows(jnp.int32(7))
    for m in (6, 7):
        for e in range(2):
            store(m % 2, e, m).wait()


def block(rows, cols, row_weight, column_weight, pair_map_weight, dilated_weight, mixing_weight):
    hbm = pl.BlockSpec(memory_space=pltpu.HBM)
    return pl.pallas_call(
        block_kernel,
        out_shape=jax.ShapeDtypeStruct((48, 256, 128), bf16),
        in_specs=[hbm] * 7,
        out_specs=hbm,
        scratch_shapes=[
            pltpu.VMEM((34, 8, 256), bf16),
            pltpu.VMEM((18, 8, 256), bf16),
            pltpu.VMEM((256, 512), bf16),
            pltpu.VMEM((256, 512), bf16),
            pltpu.VMEM((48, 512), bf16),
            pltpu.VMEM((3, 3, 48, 48), bf16),
            pltpu.VMEM((48, 48), bf16),
            pltpu.VMEM((17, 512, 128), bf16),
            pltpu.VMEM((18, 512, 128), bf16),
            pltpu.VMEM((18 * 48, 18 * 128), bf16),
            pltpu.VMEM((18 * 48, 18 * 128), bf16),
            pltpu.VMEM((144, 144), bf16),
            pltpu.VMEM((2, 2, 432, 128), f32),
            pltpu.VMEM((2, 48, 2048), bf16),
            pltpu.VMEM((2, 2, 48, 16, 128), bf16),
            pltpu.SemaphoreType.DMA((7,)),
            pltpu.SemaphoreType.DMA((2, 2)),
        ],
        compiler_params=pltpu.CompilerParams(vmem_limit_bytes=(64 << 20) - (1 << 16)),
        name="pair_block",
    )(rows, cols, row_weight, column_weight, pair_map_weight.T, dilated_weight, mixing_weight)


def on_device(trunk, row_weight, column_weight, pair_map_weight, dilated_weight, mixing_weight):
    rows, cols = gather(trunk)
    return block(rows, cols, row_weight, column_weight, pair_map_weight, dilated_weight, mixing_weight)


def solution(mesh):
    return jax.shard_map(
        on_device,
        mesh=mesh,
        in_specs=(P(("row", "col"), None), P(), P(), P(), P(), P()),
        out_specs=P(None, "row", "col"),
        check_vma=False,
    )
```

```python
import jax
import jax.numpy as jnp
from jax import lax
from jax.experimental import pallas as pl
from jax.experimental.pallas import tpu as pltpu
from jax.sharding import PartitionSpec as P

bf16 = jnp.bfloat16
f32 = jnp.float32
MESH = pl.DeviceIdType.MESH
VMEM = pl.BlockSpec(memory_space=pltpu.VMEM)


def gather_kernel(x_ref, rows_ref, cols_ref, zero_ref, send_sem, rows_sem, cols_sem):
    r = lax.axis_index("row")
    c = lax.axis_index("col")
    k = lax.rem(c, 8)
    home = 2 * r + c // 8
    barrier = pltpu.get_barrier_semaphore()
    zero_ref[...] = jnp.zeros_like(zero_ref)

    def signal(row, col):
        pl.semaphore_signal(barrier, inc=1, device_id=(row, col), device_id_type=MESH)

    def each(count, body):
        def step(n, carry):
            body(n)
            return carry

        lax.fori_loop(0, count, step, 0, unroll=True)


    @pl.when(r > 0)
    def _():
        signal(r - 1, 15)

    @pl.when(r < 7)
    def _():
        signal(r + 1, 0)

    def signal_column_source(n):
        row, col = c // 2, 8 * lax.rem(c, 2) + n

        @pl.when((row != r) | (col != c))
        def _():
            signal(row, col)

    each(8, signal_column_source)

    @pl.when(c > 0)
    def _():
        row, col = (c - 1) // 2, 8 * lax.rem(c - 1, 2) + 7

        @pl.when((row != r) | (col != c))
        def _():
            signal(row, col)

    @pl.when(c < 15)
    def _():
        row, col = (c + 1) // 2, 8 * lax.rem(c + 1, 2)

        @pl.when((row != r) | (col != c))
        def _():
            signal(row, col)

    each(15, lambda n: signal(r, lax.rem(c + 1 + n, 16)))

    low_halo_rows = (c == 15) & (r < 7)
    high_halo_rows = (c == 0) & (r > 0)
    low_halo_cols = (k == 7) & (home < 15)
    high_halo_cols = (k == 0) & (home > 0)

    def away(col):
        return 7 + (col != c).astype(jnp.int32)

    peers = 15 + away(home)
    peers += 16 * (low_halo_rows | high_halo_rows).astype(jnp.int32)
    peers += low_halo_cols.astype(jnp.int32) * away(home + 1)
    peers += high_halo_cols.astype(jnp.int32) * away(home - 1)
    pl.semaphore_wait(barrier, peers)

    def remote(src, dst, sem, row, col):
        return pltpu.make_async_remote_copy(
            src_ref=src, dst_ref=dst, send_sem=send_sem, recv_sem=sem, device_id=(row, col), device_id_type=MESH
        )

    own_rows = rows_ref.at[pl.ds(1 + 2 * c, 2)]
    own_cols = cols_ref.at[pl.ds(1 + 2 * k, 2)]

    def to_column(src, dst, col):
        def body(n):
            row = lax.rem(r + n, 8)
            other = (row != r) | (col != c)

            @pl.when(other)
            def _():
                remote(src, dst, cols_sem, row, col).start()

            @pl.when(jnp.logical_not(other))
            def _():
                pltpu.make_async_copy(src, dst, cols_sem).start()

        each(8, body)

    @pl.when(low_halo_rows)
    def _():
        each(16, lambda n: remote(x_ref.at[1], rows_ref.at[0], rows_sem, r + 1, n).start())

    @pl.when(high_halo_rows)
    def _():
        each(16, lambda n: remote(x_ref.at[0], rows_ref.at[33], rows_sem, r - 1, n).start())

    @pl.when(low_halo_cols)
    def _():
        to_column(x_ref.at[1], cols_ref.at[0], home + 1)

    @pl.when(high_halo_cols)
    def _():
        to_column(x_ref.at[0], cols_ref.at[17], home - 1)

    to_column(x_ref, own_cols, home)
    each(15, lambda n: remote(x_ref, own_rows, rows_sem, r, lax.rem(c + 1 + n, 16)).start())
    pltpu.make_async_copy(x_ref, own_rows, rows_sem).start()

    @pl.when(r == 0)
    def _():
        pltpu.make_async_copy(zero_ref, rows_ref.at[0], rows_sem).start()

    @pl.when(r == 7)
    def _():
        pltpu.make_async_copy(zero_ref, rows_ref.at[33], rows_sem).start()

    @pl.when(c == 0)
    def _():
        pltpu.make_async_copy(zero_ref, cols_ref.at[0], cols_sem).start()

    @pl.when(c == 15)
    def _():
        pltpu.make_async_copy(zero_ref, cols_ref.at[17], cols_sem).start()

    def sent(blocks):
        part = rows_ref.at[pl.ds(0, blocks)]
        pltpu.make_async_copy(part, part, send_sem).wait()

    sent(30)

    sent(14)

    @pl.when(home != c)
    def _():
        sent(2)

    @pl.when(low_halo_rows)
    def _():
        sent(16)

    @pl.when(high_halo_rows)
    def _():
        sent(16)

    def column_sent(col):
        sent(7)

        @pl.when(col != c)
        def _():
            sent(1)

    @pl.when(low_halo_cols)
    def _():
        column_sent(home + 1)

    @pl.when(high_halo_cols)
    def _():
        column_sent(home - 1)

    pltpu.make_async_copy(rows_ref, rows_ref, rows_sem).wait()
    pltpu.make_async_copy(cols_ref, cols_ref, cols_sem).wait()


def gather(trunk):
    width = trunk.shape[1]
    return pl.pallas_call(
        gather_kernel,
        out_shape=(
            jax.ShapeDtypeStruct((34, 8, width), bf16),
            jax.ShapeDtypeStruct((18, 8, width), bf16),
        ),
        in_specs=[VMEM],
        out_specs=(pl.BlockSpec(memory_space=pltpu.HBM),) * 2,
        scratch_shapes=[
            pltpu.VMEM((8, width), bf16),
            pltpu.SemaphoreType.DMA,
            pltpu.SemaphoreType.DMA,
            pltpu.SemaphoreType.DMA,
        ],
        compiler_params=pltpu.CompilerParams(collective_id=0, has_side_effects=True),
        name="gather_bins",
    )(trunk.reshape(2, 8, width))


def dot(a, b, dims=((1,), (0,))):
    return lax.dot_general(a, b, (dims, ((), ())), preferred_element_type=f32)


def block_kernel(
    rows_hbm, cols_hbm, row_w_hbm, col_w_hbm, pair_w_hbm, taps_hbm, mix_hbm, out_hbm,
    rows_in, cols_in, row_w_in, col_w_in, pair_w_in, taps_in, mix_in,
    row_pat, col_pat, act, base, taps, turn, held, out_tile, in_sem, out_sem,
):
    r = lax.axis_index("row")
    c = lax.axis_index("col")
    loads = [
        pltpu.make_async_copy(src, dst, in_sem.at[n])
        for n, (src, dst) in enumerate(
            (
                (row_w_hbm, row_w_in),
                (rows_hbm, rows_in),
                (col_w_hbm, col_w_in),
                (cols_hbm, cols_in),
                (taps_hbm, taps_in),
                (pair_w_hbm, pair_w_in),
                (mix_hbm, mix_in),
            )
        )
    ]
    for load in loads:
        load.start()

    loads[0].wait()
    row_w = row_w_in[...].T
    loads[1].wait()
    def row_patterns(n):
        cells = []
        for p in (2 * n, 2 * n + 1)[: 1 if n == 8 else 2]:
            for e in range(2):
                bins = rows_in[33 * e if p == 16 else 16 * e + p + 1].astype(f32)
                cells.append(jnp.broadcast_to(bins[:, None, :], (8, 8, 256)).reshape(64, 256))
        proj = dot(row_w, jnp.concatenate(cells, 0).astype(bf16), ((1,), (1,))).astype(bf16)
        row_pat[2 * n] = proj[:, :128]
        if n < 8:
            row_pat[2 * n + 1] = proj[:, 128:]

    row_patterns(0)
    loads[2].wait()
    col_w = col_w_in[...].T
    loads[3].wait()
    for n in range(9):
        cells = [jnp.broadcast_to(cols_in[q].astype(f32)[None], (16, 8, 256)).reshape(128, 256) for q in (2 * n, 2 * n + 1)]
        proj = dot(col_w, jnp.concatenate(cells, 0).astype(bf16), ((1,), (1,))).astype(bf16)
        col_pat[2 * n] = proj[:, :128]
        col_pat[2 * n + 1] = proj[:, 128:]
    loads[4].wait()
    for a in range(3):
        for b in range(3):
            taps[48 * b : 48 * b + 48, 48 * a : 48 * a + 48] = taps_in[a, b]
    loads[5].wait()
    loads[6].wait()

    lane = lax.broadcasted_iota(jnp.int32, (1, 128), 1)
    zero = jnp.zeros((), bf16)
    pair_w = pair_w_in[...]

    not_first = (c > 0).astype(f32)
    not_last = (c < 15).astype(f32)
    left = lane < 64

    def pair_chunk(row, n):
        pair_act = jnp.concatenate(
            [jnp.maximum(row + col_pat[2 * n], zero), jnp.maximum(row + col_pat[2 * n + 1], zero)], axis=1
        )
        hidden = dot(pair_w, pair_act)
        shown = jnp.maximum(hidden, 0.0)
        if n == 0:
            shown = jnp.concatenate([shown[:, :128] * not_first, shown[:, 128:]], axis=1)
        if n == 8:
            shown = jnp.concatenate([shown[:, :128], shown[:, 128:] * not_last], axis=1)
        return hidden, shown

    def pair_rows(p):
        row = row_pat[p]
        at = slice(48 * p + 48, 48 * p + 96)
        for n in range(9):
            hidden, shown = pair_chunk(row, n)
            act[at, 256 * n : 256 * n + 256] = shown.astype(bf16)
            base[at, 256 * n : 256 * n + 256] = hidden.astype(bf16)

    for n in range(1, 9):
        row_patterns(n)
        pair_rows(2 * n - 2)
        pair_rows(2 * n - 1)

    inside = jnp.where(left, (r > 0).astype(f32), (r < 7).astype(f32))
    inside = jnp.concatenate([inside, inside], axis=1)
    halo_row = row_pat[16]
    for n in range(9):
        halo = (pair_chunk(halo_row, n)[1] * inside).astype(bf16)
        for u in range(2):
            at = slice(256 * n + 128 * u, 256 * n + 128 * u + 128)
            outer = halo[:, 128 * u : 128 * u + 128]
            act[0:48, at] = jnp.where(left, outer, pltpu.roll(act[768:816, at], 64, 1))
            act[816:864, at] = jnp.where(left, pltpu.roll(act[48:96, at], 64, 1), outer)

    mix = mix_in[...]
    tap_w = taps[...]
    group = lane // 8

    def store(slot, e, m):
        return pltpu.make_async_copy(
            out_tile.at[slot, e], out_hbm.at[:, pl.ds(pl.multiple_of(128 * e + 16 * m, 16), 16), :], out_sem.at[slot, e]
        )

    def conv_rows(m):
        mids = []
        for u in range(2):
            at = pl.ds(pl.multiple_of(96 * m + 48 * u, 16), 144)
            sums = dot(tap_w, act[at, :])
            mids.append(jnp.maximum(sums[:48, :2048] + sums[48:96, 128:2176] + sums[96:, 256:], 0.0).astype(bf16))
        mixed = [dot(mix, mids[u]) for u in range(2)]
        for u in range(2):
            here = base[pl.ds(pl.multiple_of(96 * m + 48 * u + 48, 16), 48), 128:2176]
            held[u] = (mixed[u] + here.astype(f32)).astype(bf16)

    def turn_rows(m):
        for u in range(2):
            tiles = [held[u, :, 128 * q : 128 * q + 128] for q in range(16)]
            tiles = [pltpu.roll(tile, 8 * q, 1) if q else tile for q, tile in enumerate(tiles)]
            tiles = [tiles[-k % 16] for k in range(16)]
            for d in (1, 2, 4, 8):
                move = (group & d) != 0
                tiles = [jnp.where(move, tiles[(k - d) % 16], tiles[k]) for k in range(16)]
            tiles = [pltpu.roll(tile, 128 - 8 * k, 1) if k else tile for k, tile in enumerate(tiles)]
            for k in range(16):
                turn[k // 8, u, pl.ds(k % 8, 48, stride=9), :] = tiles[k].astype(f32)

    def pack_rows(m):
        for e in range(2):
            halves = [jnp.stack([turn[e, u, 9 * o : 9 * o + 8] for o in range(48)]) for u in range(2)]
            out_tile[lax.rem(m, 2), e] = jnp.concatenate(halves, axis=1).astype(bf16)

    def put_rows(m):
        for e in range(2):
            store(lax.rem(m, 2), e, m).start()

    def step(m, carry):
        @pl.when(m >= 3)
        def _():
            for e in range(2):
                store(lax.rem(m - 1, 2), e, m - 3).wait()

        turn_rows(m - 1)
        pack_rows(m - 1)
        conv_rows(m)
        put_rows(m - 1)
        return carry

    conv_rows(0)
    lax.fori_loop(1, 8, step, 0)
    last = jnp.int32(7)
    for e in range(2):
        store(1, e, 5).wait()
    turn_rows(last)
    pack_rows(last)
    put_rows(last)
    for m in (6, 7):
        for e in range(2):
            store(m % 2, e, m).wait()


def block(rows, cols, row_weight, column_weight, pair_map_weight, dilated_weight, mixing_weight):
    hbm = pl.BlockSpec(memory_space=pltpu.HBM)
    return pl.pallas_call(
        block_kernel,
        out_shape=jax.ShapeDtypeStruct((48, 256, 128), bf16),
        in_specs=[hbm] * 7,
        out_specs=hbm,
        scratch_shapes=[
            pltpu.VMEM((34, 8, 256), bf16),
            pltpu.VMEM((18, 8, 256), bf16),
            pltpu.VMEM((256, 512), bf16),
            pltpu.VMEM((256, 512), bf16),
            pltpu.VMEM((48, 512), bf16),
            pltpu.VMEM((3, 3, 48, 48), bf16),
            pltpu.VMEM((48, 48), bf16),
            pltpu.VMEM((17, 512, 128), bf16),
            pltpu.VMEM((18, 512, 128), bf16),
            pltpu.VMEM((18 * 48, 18 * 128), bf16),
            pltpu.VMEM((18 * 48, 18 * 128), bf16),
            pltpu.VMEM((144, 144), bf16),
            pltpu.VMEM((2, 2, 432, 128), f32),
            pltpu.VMEM((2, 48, 2048), bf16),
            pltpu.VMEM((2, 2, 48, 16, 128), bf16),
            pltpu.SemaphoreType.DMA((7,)),
            pltpu.SemaphoreType.DMA((2, 2)),
        ],
        compiler_params=pltpu.CompilerParams(vmem_limit_bytes=(64 << 20) - (1 << 16)),
        name="pair_block",
    )(rows, cols, row_weight, column_weight, pair_map_weight.T, dilated_weight, mixing_weight)


def on_device(trunk, row_weight, column_weight, pair_map_weight, dilated_weight, mixing_weight):
    rows, cols = gather(trunk)
    return block(rows, cols, row_weight, column_weight, pair_map_weight, dilated_weight, mixing_weight)


def solution(mesh):
    return jax.shard_map(
        on_device,
        mesh=mesh,
        in_specs=(P(("row", "col"), None), P(), P(), P(), P(), P()),
        out_specs=P(None, "row", "col"),
        check_vma=False,
    )
```
